32 devices in a mesh: ctx: 8 (over y, x, core), tp: 4 (over z).
Axes of the slice: x: 2, y: 2, z: 4, core: 2. Of those that a mesh axis runs over, the one named last changes fastest.
Arguments:
- patches: bfloat16 [4096, 1280], P('ctx'), may hold values from -21 to 21
- window_ids: int32 [4096], P('ctx'), may hold values from -1 to 1023, as said below
- positions: int32 [1024], P('ctx'), may hold values from 0 to 8192, as said below
- text_embed: bfloat16 [8192, 8192], P('ctx', 'tp'), may hold values from -6 to 6
- cotangent: bfloat16 [8192, 8192], P('ctx', 'tp'), may hold values from -0.119628906 to 0.119628906
- qkv_weight: bfloat16 [3, 1280, 1280], P(None, None, 'tp'), may hold values from -0.15625 to 0.15625
- out_weight: bfloat16 [1280, 1280], P('tp'), may hold values from -0.15625 to 0.15625
- merger_weight: bfloat16 [5120, 8192], P('ctx', 'tp'), may hold values from -0.078125 to 0.078125
- norm_gain: bfloat16 [8192], P('tp'), may hold values from 0.099609375 to 1.8984375
Outputs:
- normed: bfloat16 [8192, 8192], P('ctx', 'tp')
- merger_grad: float32 [5120, 8192], P('ctx', 'tp')
The draws below stay inside these ranges and needn't reach their ends.
Inputs may be any that keep to these rules, and one draw needn't show every extreme that they name: `window_ids`: windows are runs of consecutive patch slots of one index of ctx, each of 4 to 64 slots and a multiple of 4; every window id belongs to one index of ctx; the padding slots of an index of ctx come after its live slots and carry -1. Merged slot j of an index of ctx covers its patch slots 4j to 4j+3 and is live exactly when those are; live slots carry distinct positions, dead ones carry 8192. The live slots of one index of ctx name at most 16 positions among the 1024 positions of any one index of ctx.
All inputs are finite; a program needn't handle non-finite values.
Results may differ from the reference program's by a relative error of at most 0.014.
Values may be sent and summed in bfloat16 or wider, within the bound.
No kernel may reach another device: no remote copies, remote signals or barrier semaphores. Data moves between devices by JAX's collectives and lax.ppermute only.
A program may use at most 128 MiB of HBM per device.

```python
import jax
import jax.numpy as jnp
from jax import lax

DV = 1280
HEADS = 16
D = 8192
V_DEV = 512
TOK_DEV = 1024
HEAD_DIM = 80
MERGE_IN = 5120
M_DEV = 128
CAP = 16
TOKENS = 8192
N_CTX = 8


def layout(key):
    base = jax.random.fold_in(key, 7)
    keys = jax.random.split(base, 7)
    live = jnp.minimum(jax.random.randint(keys[0], (N_CTX,), M_DEV // 8, M_DEV + 1), jax.random.randint(keys[1], (N_CTX,), M_DEV // 8, M_DEV + 1))
    full_device = jax.random.randint(keys[2], (), 0, N_CTX)
    live = jnp.where(jnp.arange(N_CTX) == full_device, M_DEV, live)
    busiest = jax.random.randint(keys[3], (), 0, N_CTX)
    rest = jax.vmap(lambda k: jax.random.permutation(k, N_CTX - 1))(jax.random.split(keys[4], N_CTX))
    spread = jnp.concatenate([jnp.zeros((N_CTX, 1), jnp.int32), 1 + rest.astype(jnp.int32)], axis=1)
    row_order = jax.vmap(lambda k: jax.random.permutation(k, TOK_DEV))(jax.random.split(keys[5], N_CTX)).astype(jnp.int32)
    source = jnp.arange(N_CTX, dtype=jnp.int32)[:, None]
    slot = jnp.arange(M_DEV, dtype=jnp.int32)[None, :]
    group = slot // CAP
    within = slot % CAP
    target = (busiest + jnp.take_along_axis(spread, jnp.broadcast_to(group, (N_CTX, M_DEV)), axis=1)) % N_CTX
    local_row = row_order[target, source * CAP + within]
    alive = slot < live[:, None]
    positions = jnp.where(alive, target * TOK_DEV + local_row, TOKENS).reshape(-1).astype(jnp.int32)
    lengths = jax.random.randint(keys[6], (N_CTX, M_DEV), 1, 17)
    ends = jnp.cumsum(lengths, axis=1)
    window_of_unit = jnp.sum((ends[:, None, :] <= slot[:, :, None]).astype(jnp.int32), axis=2)
    unit_ids = jnp.where(alive, source * M_DEV + window_of_unit, -1)
    window_ids = jnp.repeat(unit_ids, 4, axis=1).reshape(-1).astype(jnp.int32)
    return (window_ids, positions)


def draw_window_ids(key, part):
    return layout(key)[0]


def draw_positions(key, part):
    return layout(key)[1]


def draw_patches(key, part):
    base = jax.random.fold_in(key, 11)
    keys = jax.random.split(base, 1)
    values = jnp.clip(jax.random.normal(keys[0], (N_CTX * V_DEV, DV), jnp.float32), -6.0, 6.0)
    return values.astype(jnp.bfloat16)


def block_scale(rng, extent, cuts, smallest, high):
    level = 1.0
    for position, shards_of in cuts:
        draws = jax.random.uniform(jax.random.fold_in(jax.random.fold_in(rng, 6), position), (shards_of,), jnp.float32, smallest / len(cuts), high / len(cuts))
        level = level * jnp.repeat(jnp.exp(draws), extent[position] // shards_of).reshape((-1,) + (1,) * (len(extent) - 1 - position))
    return level


def scatter_about(key, dims, deviation, limit, cuts=(), held_as=jnp.bfloat16):
    result = jax.random.normal(key, dims, jnp.float32) * deviation
    if len(cuts) > 0:
        result = block_scale(key, dims, cuts, -0.22, 0.18) * result
    return jnp.clip(result, min=-limit, max=limit).astype(held_as)


def setup_inputs(seed: int = 0) -> dict:
    splits = jax.random.split(jax.random.key(seed), 10)
    patches = draw_patches(jax.random.fold_in(splits[9], 71), 0)
    window_ids = draw_window_ids(jax.random.fold_in(splits[9], 71), 0)
    positions = draw_positions(jax.random.fold_in(splits[9], 71), 0)
    text_embed = scatter_about(splits[3], (TOKENS, D), 1.0, 6.0, ((0, 8), (1, 4)))
    cotangent = scatter_about(splits[4], (TOKENS, D), 0.02, 0.119628906, ((0, 8), (1, 4)))
    qkv_weight = scatter_about(splits[5], (3, DV, DV), DV ** -0.5, 0.15625, ((2, 4),))
    out_weight = scatter_about(splits[6], (DV, DV), DV ** -0.5, 0.15625, ((0, 4),))
    merger_weight = scatter_about(splits[7], (MERGE_IN, D), MERGE_IN ** -0.5, 0.078125, ((0, 8), (1, 4)))
    norm_gain = jnp.clip(1.0 + 0.18 * jax.random.normal(splits[8], (D,), jnp.float32), 0.099609375, 1.8984375).astype(jnp.bfloat16)
    return dict(patches=patches, window_ids=window_ids, positions=positions, text_embed=text_embed, cotangent=cotangent, qkv_weight=qkv_weight, out_weight=out_weight, merger_weight=merger_weight, norm_gain=norm_gain)


def attend(block_x, block_ids, qkv_weight, out_weight):
    projected = [jnp.dot(block_x, qkv_weight[i], preferred_element_type=jnp.float32).astype(jnp.bfloat16) for i in range(3)]
    queries = projected[0].reshape(V_DEV, HEADS, HEAD_DIM)
    keys_all = projected[1].reshape(V_DEV, HEADS, HEAD_DIM)
    values = projected[2].reshape(V_DEV, HEADS, HEAD_DIM)
    width = min(512, V_DEV)
    factor = 1.0 / HEAD_DIM ** 0.5

    def one_block(block_index):
        first_row = block_index * width
        query_rows = lax.dynamic_slice_in_dim(queries, first_row, width, 0)
        query_ids = lax.dynamic_slice_in_dim(block_ids, first_row, width, 0)
        scores = jnp.einsum('qhd,khd->hqk', query_rows.astype(jnp.float32), keys_all.astype(jnp.float32)) * factor
        allowed = (query_ids[:, None] == block_ids[None, :]) & (block_ids[None, :] >= 0)
        scores = jnp.where(allowed[None], scores, jnp.float32(-1e+30))
        highest = lax.optimization_barrier(jnp.max(scores, axis=2, keepdims=True))
        weights = jnp.exp(scores - highest)
        probs = (weights / lax.optimization_barrier(jnp.sum(weights, axis=2, keepdims=True))).astype(jnp.bfloat16)
        attended = jnp.einsum('hqk,khd->qhd', probs.astype(jnp.float32), values.astype(jnp.float32))
        return attended.astype(jnp.bfloat16).reshape(width, DV)
    attended = lax.map(one_block, jnp.arange(V_DEV // width, dtype=jnp.int32)).reshape(V_DEV, DV)
    output = jnp.dot(attended, out_weight, preferred_element_type=jnp.float32)
    return (block_x.astype(jnp.float32) + output).astype(jnp.bfloat16)

def norm_rows(rows_x, rows_cot, gain):
    values = rows_x.astype(jnp.float32)
    gained = gain.astype(jnp.float32)[None, :] * rows_cot.astype(jnp.float32)
    squares = lax.optimization_barrier(jnp.sum(values * values, axis=1))
    inner = lax.optimization_barrier(jnp.sum(values * gained, axis=1))
    scale = lax.rsqrt(squares / D + 1e-06)[:, None]
    normed = (values * scale * gain.astype(jnp.float32)[None, :]).astype(jnp.bfloat16)
    d_embed = (scale * gained - values * scale ** 3 * inner[:, None] / D).astype(jnp.bfloat16)
    return (normed, d_embed)

def reference(patches, window_ids, positions, text_embed, cotangent, qkv_weight, out_weight, merger_weight, norm_gain):
    grouped = patches.reshape(N_CTX, V_DEV, DV)
    grouped_ids = window_ids.reshape(N_CTX, V_DEV)
    hidden = lax.map(lambda pair: attend(pair[0], pair[1], qkv_weight, out_weight), (grouped, grouped_ids))
    merged_in = hidden.reshape(N_CTX * M_DEV, MERGE_IN)
    merged = jnp.dot(merged_in, merger_weight, preferred_element_type=jnp.float32).astype(jnp.bfloat16)
    embedded = text_embed.at[positions].set(merged, mode='drop')
    normed, d_embed = lax.map(lambda pair: norm_rows(pair[0], pair[1], norm_gain), (embedded.reshape(N_CTX, TOK_DEV, D), cotangent.reshape(N_CTX, TOK_DEV, D)))
    normed = normed.reshape(TOKENS, D)
    d_embed = d_embed.reshape(TOKENS, D)
    d_merged = jnp.take(d_embed, positions, axis=0, mode='fill', fill_value=0)
    merger_grad = jnp.dot(merged_in.T, d_merged, preferred_element_type=jnp.float32)
    return (normed, merger_grad)
```

```python
import jax
import jax.numpy as jnp
from jax import lax
from jax.sharding import PartitionSpec as P

D = 8192
HEAD_DIM = 80
BF = jnp.bfloat16
F32 = jnp.float32


def dot(a, b):
    return jnp.dot(a, b, preferred_element_type=F32)


def contract_rows(left, right):
    return lax.dot_general(left, right, (((0,), (0,)), ((), ())), preferred_element_type=F32)


def swap(x, axis, mask):
    size = lax.axis_size(axis)
    return lax.ppermute(x, axis, [(i, i ^ mask) for i in range(size)])


def window_attention(patches, window_ids, qkv_weight):
    rows = patches.shape[0]
    heads = qkv_weight.shape[2] // HEAD_DIM
    q, k, v = [dot(patches, qkv_weight[i]).astype(BF).reshape(rows, heads, HEAD_DIM) for i in range(3)]
    scores = jnp.einsum("qhd,khd->hqk", q, k, preferred_element_type=F32) * (1.0 / HEAD_DIM**0.5)
    allowed = (window_ids[:, None] == window_ids[None, :]) & (window_ids[None, :] >= 0)
    scores = jnp.where(allowed[None], scores, F32(-1e30))
    weights = jnp.exp(scores - jnp.max(scores, axis=2, keepdims=True))
    probs = (weights / jnp.sum(weights, axis=2, keepdims=True)).astype(BF)
    attended = jnp.einsum("hqk,khd->qhd", probs, v, preferred_element_type=F32)
    return attended.astype(BF).reshape(rows, heads * HEAD_DIM)


def block_order(bits):
    order = [0]
    for bit in bits:
        order = [i | j for i in order for j in (0, bit)]
    return order


def exchange(x, bits):
    x = x[:, None]
    senders = [0]
    for bit in bits:
        half = x.shape[0] // 2
        x = jnp.concatenate([x[:half], swap(x[half:], "ctx", bit)], axis=1)
        senders = senders + [s ^ bit for s in senders]
    return x[0], senders


def gather_bits(blocks, bits):
    for bit in bits:
        keys = list(blocks)
        got = swap(jnp.stack([blocks[k] for k in keys]), "ctx", bit)
        blocks = {**blocks, **{k ^ bit: got[i] for i, k in enumerate(keys)}}
    return blocks


def gather_tp(x, t):
    size = lax.axis_size("tp")
    if size != 4:
        return [x] + [swap(x, "tp", r) for r in range(1, size)]
    near, far = swap(x, "tp", 1), swap(x, "tp", 2)
    x, near, far = lax.optimization_barrier((x, near, far))
    middle = lax.ppermute(x, "tp", [(1, 2), (2, 1)])
    ends = lax.ppermute(far, "tp", [(1, 0), (2, 3)])
    return [x, near, far, jnp.where((t == 0) | (t == 3), ends, middle)]


def sum_tp(x):
    size = lax.axis_size("tp")
    total = x
    for r in range(1, size):
        total = total + swap(x, "tp", r)
    return total


def shards(
    patches, window_ids, positions, text_embed, cotangent, qkv_weight, out_weight, merger_weight, norm_gain
):
    n = lax.axis_size("ctx")
    tp_size = lax.axis_size("tp")
    chips = n // 2
    c, t = lax.axis_index("ctx"), lax.axis_index("tp")
    chip, core = c // 2, c % 2
    slots, tok_rows = positions.shape[0], text_embed.shape[0]
    features = text_embed.shape[1]
    dv = patches.shape[1]
    own_cols = merger_weight.shape[0]
    group = n * own_cols // dv
    share = chips // group
    cap = slots // n
    ctx_bits = [1 << i for i in range((n - 1).bit_length())]
    chip_bits = ctx_bits[:-1]
    flipped = [1] + ctx_bits[:0:-1]

    target = positions // tok_rows
    earlier = jnp.arange(slots)[:, None] > jnp.arange(slots)[None, :]
    rank = jnp.sum((earlier & (target[:, None] == target[None, :])).astype(jnp.int32), axis=1)
    key = jnp.where(target < n, target * cap + rank, -1)

    receivers = jnp.array(block_order(ctx_bits), jnp.int32)[:, None, None]
    rel_chip = jnp.arange(chips, dtype=jnp.int32)[None, :, None]
    ranks = jnp.arange(cap, dtype=jnp.int32)[None, None, :]
    receiver = c ^ receivers
    wanted = ((receiver // 2 ^ rel_chip) * 2 + receiver % 2) * cap + ranks
    wanted = (wanted * group + receiver // 2 // share).reshape(-1)
    slot_key = jnp.where(key[:, None] >= 0, key[:, None] * group + jnp.arange(group)[None, :], -1).reshape(-1)
    select = (wanted[:, None] == slot_key[None, :]).astype(BF)

    def arrange(blocks, senders):
        blocks = blocks.reshape(n, chips, cap, blocks.shape[-1])
        parts = [blocks[senders.index(s ^ (2 * r)), r] for r in range(chips) for s in range(n)]
        return jnp.concatenate(parts, axis=0)

    attended = window_attention(patches, window_ids, qkv_weight)
    att_out = dot(select, attended).astype(BF).reshape(n, chips * cap, -1)
    att_mine = arrange(*exchange(att_out, ctx_bits))
    att_all = gather_tp(att_mine, t)

    piece_rows = out_weight.shape[0] // n
    piece = lax.dynamic_slice_in_dim(out_weight, c * piece_rows, piece_rows, 0)
    pieces = jnp.stack([piece] + [swap(piece, "tp", r) for r in range(1, tp_size)])
    pieces, att_out_dep = lax.optimization_barrier((pieces, att_mine))
    got = gather_bits({0: pieces}, ctx_bits[1:] + [1])
    by_rel = jnp.stack([got[r] for r in range(n)])
    by_abs = [lax.dynamic_index_in_dim(by_rel, c ^ i, 0, keepdims=False) for i in range(n)]
    out_full = jnp.stack(by_abs, axis=1).reshape(tp_size, n * piece_rows, dv)

    pat_out = dot(select, patches).astype(BF).reshape(n, chips * cap, dv)
    first = (chip % share) * 2 * own_cols
    if share > 1:
        pat_out = jnp.stack(
            [
                lax.dynamic_slice_in_dim(pat_out[i], ((c ^ r) // 2 % share) * 2 * own_cols, 2 * own_cols, 1)
                for i, r in enumerate(block_order(ctx_bits))
            ]
        )
    pat_mine = arrange(*exchange(pat_out, ctx_bits))

    def hidden_cols(which):
        start = which * own_cols
        weight = lax.dynamic_slice_in_dim(out_full, first + start, own_cols, 2)
        total = lax.dynamic_slice_in_dim(pat_mine, start, own_cols, 1).astype(F32)
        for r in range(tp_size):
            total = total + dot(att_all[r], weight[r])
        return total.astype(BF)

    hidden_own, hidden_other = hidden_cols(core), hidden_cols(1 - core)
    hidden = jnp.concatenate([hidden_own, hidden_other], axis=1).reshape(chips, slots, 2 * own_cols)
    weight_chip = jnp.concatenate([merger_weight, swap(merger_weight, "ctx", 1)], axis=0)

    half = features // 2
    arrived = []
    for cols, bits in ((weight_chip[:, :half], chip_bits), (weight_chip[:, half:], chip_bits[::-1])):
        bit = bits[0]
        keep_ids = [r for r in range(chips) if not r & bit]
        send = dot(jnp.concatenate([hidden[r | bit] for r in keep_ids]), cols).astype(BF)
        got = swap(send, "ctx", 2 * bit)
        keep = dot(jnp.concatenate([hidden[r] for r in keep_ids]), cols)
        total = {r: (keep + got.astype(F32)).reshape(-1, slots, half)[i] for i, r in enumerate(keep_ids)}
        for bit in bits[1:]:
            keep_ids = [r for r in total if not r & bit]
            send = jnp.stack([total[r | bit] for r in keep_ids]).astype(BF)
            got = swap(send, "ctx", 2 * bit)
            total = {r: total[r] + got[i].astype(F32) for i, r in enumerate(keep_ids)}
        arrived.append(total[0].astype(BF))
    incoming = jnp.concatenate(arrived, axis=1)

    dest = (c ^ jnp.array(block_order(ctx_bits), jnp.int32))[:, None] * cap + jnp.arange(cap)[None, :]
    hit = dest[:, :, None] == key[None, None, :]
    local_row = (positions % tok_rows)[None, None, :]
    out_rows = jnp.where(jnp.any(hit, axis=2), jnp.sum(jnp.where(hit, local_row, 0), axis=2), -1)
    in_rows = exchange(out_rows[:, None, :], ctx_bits)[0].reshape(-1)
    placed = jnp.arange(tok_rows, dtype=jnp.int32)[:, None] == in_rows[None, :]
    placed_mat = placed.astype(BF)
    is_vision = jnp.any(placed, axis=1)
    cot_rows = contract_rows(placed_mat, cotangent)

    gain = norm_gain.astype(F32)[None, :]
    text = text_embed.astype(F32)
    text_squares = sum_tp(jnp.sum(text * text, axis=1))
    text_scale = lax.rsqrt(text_squares / D + 1e-06)[:, None]

    x = incoming.astype(F32)
    gained = gain * cot_rows
    sums = sum_tp(jnp.stack([jnp.sum(x * x, axis=1), jnp.sum(x * gained, axis=1)]))
    scale = lax.rsqrt(sums[0] / D + 1e-06)[:, None]
    d_rows = (scale * gained - x * scale**3 * sums[1][:, None] / D).astype(BF)
    vision = dot(placed_mat, (x * scale * gain).astype(BF))
    normed = jnp.where(is_vision[:, None], vision, text * text_scale * gain).astype(BF)

    low = gather_bits({0: d_rows[:, :half]}, [2 * b for b in chip_bits[::-1]] + [1])
    high = gather_bits({0: d_rows[:, half:]}, [2 * b for b in chip_bits] + [1])
    keys = [2 * r + k for k in (0, 1) for r in range(chips)]
    d_all = jnp.concatenate(
        [jnp.concatenate([low[k] for k in keys]), jnp.concatenate([high[k] for k in keys])], axis=1
    )
    columns = jnp.concatenate([hidden_own, swap(hidden_other, "ctx", 1)], axis=0)
    merger_grad = contract_rows(columns, d_all)
    return (normed, merger_grad)


def solution(mesh):
    in_specs = (
        P("ctx", None),
        P("ctx"),
        P("ctx"),
        P("ctx", "tp"),
        P("ctx", "tp"),
        P(None, None, "tp"),
        P("tp", None),
        P("ctx", "tp"),
        P("tp"),
    )
    out_specs = (P("ctx", "tp"), P("ctx", "tp"))
    return jax.shard_map(shards, mesh=mesh, in_specs=in_specs, out_specs=out_specs, check_vma=False)
```

```python
import functools

import jax
import jax.numpy as jnp
from jax import lax
from jax.experimental import pallas as pl
from jax.experimental.pallas import tpu as pltpu
from jax.sharding import PartitionSpec as P

D = 8192
HEAD_DIM = 80
BF = jnp.bfloat16
F32 = jnp.float32


def dot(a, b):
    return jnp.dot(a, b, preferred_element_type=F32)


def contract_rows(left, right):
    return lax.dot_general(left, right, (((0,), (0,)), ((), ())), preferred_element_type=F32)


def swap(x, axis, mask):
    size = lax.axis_size(axis)
    return lax.ppermute(x, axis, [(i, i ^ mask) for i in range(size)])


def nt(a, b):
    return lax.dot_general(a, b, (((1,), (1,)), ((), ())), preferred_element_type=F32)


def log2(size):
    assert size & (size - 1) == 0
    return size.bit_length() - 1


def as_column(row):
    size = row.shape[1]
    eye = lax.broadcasted_iota(jnp.int32, (size, size), 0) == lax.broadcasted_iota(jnp.int32, (size, size), 1)
    return jnp.sum(jnp.where(eye, row.astype(F32), 0.0), axis=1, keepdims=True)


def attention_kernel(n, group, tok_rows, me, positions, ids, patches_hbm, qkv_hbm, *refs):
    outs, (select_out, patches, qkv, attended, sems) = refs[:n], refs[n:]
    copies = [pltpu.make_async_copy(patches_hbm, patches, sems.at[0])]
    copies += [pltpu.make_async_copy(qkv_hbm.at[i], qkv.at[i], sems.at[1 + i]) for i in range(3)]
    for copy in copies:
        copy.start()
    c = me[0]
    slots, rows = positions.shape[1], ids.shape[1]
    chips, cap, share = n // 2, slots // n, n // 2 // group

    place = positions[...]
    target = jnp.zeros_like(place)
    for i in range(1, n + 1):
        target = target + (place >= i * tok_rows).astype(jnp.int32)
    earlier = lax.broadcasted_iota(jnp.int32, (slots, slots), 0) < lax.broadcasted_iota(jnp.int32, (slots, slots), 1)
    same = as_column(target) == target.astype(F32)
    rank = jnp.sum(jnp.where(earlier & same, 1.0, 0.0), axis=0, keepdims=True).astype(jnp.int32)
    key = jnp.where(target < n, target * cap + rank, -1)

    per = chips * cap
    row = lax.broadcasted_iota(jnp.int32, (n * per, 1), 0)
    receiver = c ^ (row >> log2(per))
    chip = receiver >> 1
    wanted = (((chip ^ ((row & (per - 1)) >> log2(cap))) * 2 + (receiver & 1)) << log2(cap)) + (row & (cap - 1))
    slot_pick = (wanted == key).astype(BF)
    spread = lax.broadcasted_iota(jnp.int32, (slots, rows), 0) == (
        lax.broadcasted_iota(jnp.int32, (slots, rows), 1) >> log2(group)
    )
    offset = chip >> log2(share) == (lax.broadcasted_iota(jnp.int32, (1, rows), 1) & (group - 1))
    select = jnp.where(offset, dot(slot_pick, spread.astype(BF)), 0.0).astype(BF)
    select_out[...] = select

    ids_row = ids[...]
    ids_col = as_column(ids_row)
    allowed = (ids_col == ids_row.astype(F32)) & (ids_col >= 0)
    copies[0].wait()
    x = patches[...]
    heads = []
    for i in range(3):
        copies[1 + i].wait()
        heads.append(nt(qkv[i], x).astype(BF))
    q, k, v = heads
    width = qkv.shape[1]
    for h in range(width // HEAD_DIM):
        part = slice(h * HEAD_DIM, (h + 1) * HEAD_DIM)
        scores = lax.dot_general(k[part], q[part], (((0,), (0,)), ((), ())), preferred_element_type=F32)
        scores = jnp.where(allowed, scores * (1.0 / HEAD_DIM**0.5), F32(-1e30))
        weights = jnp.exp(scores - jnp.max(scores, axis=0, keepdims=True))
        total = jnp.sum(weights, axis=0, keepdims=True)
        attended[part] = (dot(v[part], weights.astype(BF)) / total).astype(BF)
    att = attended[...]
    none = jnp.zeros_like(att)
    left, right = jnp.concatenate([att, none], axis=0), jnp.concatenate([none, att], axis=0)
    half = per // 2
    for i in range(n):
        low, high = select[i * per : i * per + half], select[i * per + half : (i + 1) * per]
        outs[i][...] = (nt(low, left) + nt(high, right)).astype(BF)


def attention(patches, window_ids, positions, qkv_weight, c, n, group, tok_rows):
    rows, dv = patches.shape
    slots, width = positions.shape[0], qkv_weight.shape[2]
    per = n // 2 * (slots // n)
    vmem, hbm = pl.BlockSpec(memory_space=pltpu.VMEM), pl.BlockSpec(memory_space=pltpu.HBM)
    *blocks, select = pl.pallas_call(
        functools.partial(attention_kernel, n, group, tok_rows),
        in_specs=[pl.BlockSpec(memory_space=pltpu.SMEM), vmem, vmem, hbm, hbm],
        out_specs=[vmem] * (n + 1),
        out_shape=[jax.ShapeDtypeStruct((per // 2, 2 * width), BF)] * n + [jax.ShapeDtypeStruct((n * per, rows), BF)],
        scratch_shapes=[
            pltpu.VMEM((rows, dv), BF),
            pltpu.VMEM((3, width, dv), BF),
            pltpu.VMEM((width, rows), BF),
            pltpu.SemaphoreType.DMA((4,)),
        ],
        compiler_params=pltpu.CompilerParams(vmem_limit_bytes=48 * 1024 * 1024),
        name="attention",
    )(c.reshape(1), positions[None, :], window_ids[None, :], patches, jnp.swapaxes(qkv_weight, 1, 2))
    return blocks, select


def project_kernel(n, cap, first, last, *refs):
    count = last - first
    atts, weights, rest = refs[:count], refs[count : 3 * count], refs[3 * count :]
    base, outs, (arranged, padded) = rest[:2], rest[2:4], rest[4:]
    chips = n // 2
    half = chips // 2
    width = weights[0].shape[0]
    size = half * n * cap
    blank = jnp.zeros((width, weights[0].shape[1]), BF)
    padded[:width] = blank
    padded[2 * width :] = blank
    totals = [[None, None], [None, None]]
    for i in range(count):
        for j in range(half):
            for p in range(n):
                s = p ^ (2 * j)
                arranged[(j * n + p) * cap : (j * n + p + 1) * cap] = atts[i][(s * half + j) * cap : (s * half + j + 1) * cap]
        rows = arranged[...]
        for side in range(2):
            padded[width : 2 * width] = weights[2 * i + side][...]
            for h, start in ((0, width), (1, 0)):
                part = dot(rows, padded[start : start + 2 * width])
                totals[side][h] = part if totals[side][h] is None else totals[side][h] + part
    for side in range(2):
        for h in range(2):
            if first == 0:
                start = base[side][h * size : (h + 1) * size].astype(F32)
            else:
                start = base[side][h * size : (h + 1) * size]
            total = start + totals[side][h]
            if first == 0:
                outs[side][h * size : (h + 1) * size] = total
                continue
            turn = n // 2 * cap if h else 0
            for j in range(half):
                block = total[j * n * cap : (j + 1) * n * cap].astype(BF)
                at = (h * half + j) * n * cap
                if turn:
                    outs[side][at : at + turn] = block[turn:]
                    outs[side][at + turn : at + n * cap] = block[:turn]
                else:
                    outs[side][at : at + n * cap] = block


def project(atts, weights, base, n, cap, first, last, dtype):
    rows, cols = base[0].shape
    width = weights[0].shape[0]
    return pl.pallas_call(
        functools.partial(project_kernel, n, cap, first, last),
        out_shape=[jax.ShapeDtypeStruct((rows, cols), dtype)] * 2,
        scratch_shapes=[pltpu.VMEM((rows // 2, 2 * width), BF), pltpu.VMEM((3 * width, cols), BF)],
        compiler_params=pltpu.CompilerParams(vmem_limit_bytes=48 * 1024 * 1024),
        name="project_all" if first == 0 else "project_last",
    )(*atts, *weights, *base)


def block_order(bits):
    order = [0]
    for bit in bits:
        order = [i | j for i in order for j in (0, bit)]
    return order


def exchange(x, bits):
    x = x[:, None]
    senders = [0]
    for bit in bits:
        half = x.shape[0] // 2
        x = jnp.concatenate([x[:half], swap(x[half:], "ctx", bit)], axis=1)
        senders = senders + [s ^ bit for s in senders]
    return x[0], senders


def gather_bits(blocks, bits):
    for bit in bits:
        keys = list(blocks)
        got = swap(jnp.stack([blocks[k] for k in keys]), "ctx", bit)
        blocks = {**blocks, **{k ^ bit: got[i] for i, k in enumerate(keys)}}
    return blocks


def gather_tp(x, t):
    size = lax.axis_size("tp")
    if size != 4:
        return [x] + [swap(x, "tp", r) for r in range(1, size)]
    near, far = swap(x, "tp", 1), swap(x, "tp", 2)
    x, near, far = lax.optimization_barrier((x, near, far))
    middle = lax.ppermute(x, "tp", [(1, 2), (2, 1)])
    ends = lax.ppermute(far, "tp", [(1, 0), (2, 3)])
    return [x, near, far, jnp.where((t == 0) | (t == 3), ends, middle)]


def sum_tp(x):
    size = lax.axis_size("tp")
    total = x
    for r in range(1, size):
        total = total + swap(x, "tp", r)
    return total


def shards(
    patches, window_ids, positions, text_embed, cotangent, qkv_weight, out_weight, merger_weight, norm_gain
):
    n = lax.axis_size("ctx")
    tp_size = lax.axis_size("tp")
    chips = n // 2
    c, t = lax.axis_index("ctx"), lax.axis_index("tp")
    chip, core = c // 2, c % 2
    slots, tok_rows = positions.shape[0], text_embed.shape[0]
    features = text_embed.shape[1]
    dv = patches.shape[1]
    own_cols = merger_weight.shape[0]
    group = n * own_cols // dv
    share = chips // group
    cap = slots // n
    ctx_bits = [1 << i for i in range((n - 1).bit_length())]
    chip_bits = ctx_bits[:-1]

    blocks, select = attention(patches, window_ids, positions, qkv_weight, c, n, group, tok_rows)
    att_mine = jnp.concatenate([blocks[0]] + [swap(blocks[s], "ctx", s) for s in range(1, n)], axis=0)
    att_all = gather_tp(att_mine, t)

    piece_rows = out_weight.shape[0] // n
    out_weight, _ = lax.optimization_barrier((out_weight, select))
    piece = lax.dynamic_slice_in_dim(out_weight, c * piece_rows, piece_rows, 0)
    pieces = jnp.stack([piece] + [swap(piece, "tp", r) for r in range(1, tp_size)])
    pieces, _ = lax.optimization_barrier((pieces, att_mine))
    mid = dv // 2
    left = gather_bits({0: pieces[..., :mid]}, ctx_bits[1:] + [1])
    right = gather_bits({0: pieces[..., mid:]}, ctx_bits[:0:-1] + [1])
    first = (chip % share) * 2 * own_cols

    def out_cols(which):
        start = first + which * own_cols
        by_rel = jnp.stack([jnp.concatenate([left[r], right[r]], axis=2) for r in range(n)])
        by_rel = lax.dynamic_slice_in_dim(by_rel, start, own_cols, 3)
        by_abs = [lax.dynamic_index_in_dim(by_rel, c ^ i, 0, keepdims=False) for i in range(n)]
        return jnp.stack(by_abs, axis=1).reshape(tp_size, n * piece_rows, own_cols)

    out_own, out_other = out_cols(core), out_cols(1 - core)

    pat_out = dot(select, patches).astype(BF).reshape(n, chips * cap, dv)
    if share > 1:
        pat_out = jnp.stack(
            [
                lax.dynamic_slice_in_dim(pat_out[r], ((c ^ r) // 2 % share) * 2 * own_cols, 2 * own_cols, 1)
                for r in range(n)
            ]
        )
    pat_mine = []
    for i, bits in enumerate((ctx_bits, [1] + ctx_bits[:0:-1])):
        part = pat_out[:, :, i * own_cols : (i + 1) * own_cols]
        part, senders = exchange(jnp.stack([part[r] for r in block_order(bits)]), bits)
        pat_mine.append((part.reshape(n, chips, cap, own_cols), senders))

    def pat_cols(i):
        part, senders = pat_mine[i]
        half = chips // 2
        rows = [
            part[senders.index(p ^ (2 * j)), h * half + j] for h in range(2) for j in range(half) for p in range(n)
        ]
        return jnp.concatenate(rows, axis=0)

    pat_abs = [pat_cols(0), pat_cols(1)]
    pat_own = jnp.where(core == 0, pat_abs[0], pat_abs[1])
    pat_other = jnp.where(core == 0, pat_abs[1], pat_abs[0])

    weights = [w for r in range(tp_size) for w in (out_own[r], out_other[r])]
    before = tp_size - 1
    so_far = project(att_all[:before], weights[: 2 * before], [pat_own, pat_other], n, cap, 0, before, F32)
    hidden_own, hidden_other = project(att_all[before:], weights[2 * before :], so_far, n, cap, before, tp_size, BF)
    hidden = jnp.concatenate([hidden_own, hidden_other], axis=1).reshape(chips, slots, 2 * own_cols)
    weight_chip = jnp.concatenate([merger_weight, swap(merger_weight, "ctx", 1)], axis=0)

    half = features // 2
    arrived = []
    for cols, bits in ((weight_chip[:, :half], chip_bits), (weight_chip[:, half:], chip_bits[::-1])):
        bit = bits[0]
        keep_ids = [r for r in range(chips) if not r & bit]
        send = dot(jnp.concatenate([hidden[r | bit] for r in keep_ids]), cols).astype(BF)
        got = swap(send, "ctx", 2 * bit)
        keep = dot(jnp.concatenate([hidden[r] for r in keep_ids]), cols)
        total = {r: (keep + got.astype(F32)).reshape(-1, slots, half)[i] for i, r in enumerate(keep_ids)}
        for bit in bits[1:]:
            keep_ids = [r for r in total if not r & bit]
            send = jnp.stack([total[r | bit] for r in keep_ids]).astype(BF)
            got = swap(send, "ctx", 2 * bit)
            total = {r: total[r] + got[i].astype(F32) for i, r in enumerate(keep_ids)}
        arrived.append(total[0].astype(BF))
    incoming = jnp.concatenate(arrived, axis=1)

    target = positions // tok_rows
    earlier = jnp.arange(slots)[:, None] > jnp.arange(slots)[None, :]
    rank = jnp.sum((earlier & (target[:, None] == target[None, :])).astype(jnp.int32), axis=1)
    key = jnp.where(target < n, target * cap + rank, -1)
    dest = (c ^ jnp.array(block_order(ctx_bits), jnp.int32))[:, None] * cap + jnp.arange(cap)[None, :]
    hit = dest[:, :, None] == key[None, None, :]
    local_row = (positions % tok_rows)[None, None, :]
    out_rows = jnp.where(jnp.any(hit, axis=2), jnp.sum(jnp.where(hit, local_row, 0), axis=2), -1)
    in_rows = exchange(out_rows[:, None, :], ctx_bits)[0].reshape(-1)
    placed = jnp.arange(tok_rows, dtype=jnp.int32)[:, None] == in_rows[None, :]
    placed_mat = placed.astype(BF)
    is_vision = jnp.any(placed, axis=1)
    cot_rows = contract_rows(placed_mat, cotangent)

    gain = norm_gain.astype(F32)[None, :]
    text = text_embed.astype(F32)
    x = incoming.astype(F32)
    gained = gain * cot_rows
    sums = [jnp.sum(text * text, axis=1), jnp.sum(x * x, axis=1), jnp.sum(x * gained, axis=1)]
    sums = sum_tp(jnp.concatenate(sums).reshape(-1, 128)).reshape(-1)
    text_scale = lax.rsqrt(sums[:tok_rows] / D + 1e-06)[:, None]
    scale = lax.rsqrt(sums[tok_rows : tok_rows + slots] / D + 1e-06)[:, None]
    inner = sums[tok_rows + slots :][:, None]
    d_rows = (scale * gained - x * scale**3 * inner / D).astype(BF)
    vision = dot(placed_mat, (x * scale * gain).astype(BF))
    normed = jnp.where(is_vision[:, None], vision, text * text_scale * gain).astype(BF)

    low = gather_bits({0: d_rows[:, :half]}, [2 * b for b in chip_bits[::-1]] + [1])
    high = gather_bits({0: d_rows[:, half:]}, [2 * b for b in chip_bits] + [1])
    keys = [2 * r + k for k in (0, 1) for r in range(chips)]
    d_all = jnp.concatenate(
        [jnp.concatenate([low[k] for k in keys]), jnp.concatenate([high[k] for k in keys])], axis=1
    )
    columns = jnp.concatenate([hidden_own, swap(hidden_other, "ctx", 1)], axis=0)
    merger_grad = contract_rows(columns, d_all)
    return (normed, merger_grad)


def solution(mesh):
    in_specs = (
        P("ctx", None),
        P("ctx"),
        P("ctx"),
        P("ctx", "tp"),
        P("ctx", "tp"),
        P(None, None, "tp"),
        P("tp", None),
        P("ctx", "tp"),
        P("tp"),
    )
    out_specs = (P("ctx", "tp"), P("ctx", "tp"))
    return jax.shard_map(shards, mesh=mesh, in_specs=in_specs, out_specs=out_specs, check_vma=False)
```

```python
import functools

import jax
import jax.numpy as jnp
from jax import lax
from jax.experimental import pallas as pl
from jax.experimental.pallas import tpu as pltpu
from jax.sharding import PartitionSpec as P


D = 8192
HEAD_DIM = 80
BF = jnp.bfloat16
F32 = jnp.float32


def dot(a, b):
    return jnp.dot(a, b, preferred_element_type=F32)


def contract_rows(left, right):
    return lax.dot_general(left, right, (((0,), (0,)), ((), ())), preferred_element_type=F32)


def swap(x, axis, mask):
    size = lax.axis_size(axis)
    return lax.ppermute(x, axis, [(i, i ^ mask) for i in range(size)])


def nt(a, b):
    return lax.dot_general(a, b, (((1,), (1,)), ((), ())), preferred_element_type=F32)


def log2(size):
    assert size & (size - 1) == 0
    return size.bit_length() - 1


def as_column(row):
    size = row.shape[1]
    eye = lax.broadcasted_iota(jnp.int32, (size, size), 0) == lax.broadcasted_iota(jnp.int32, (size, size), 1)
    return jnp.sum(jnp.where(eye, row.astype(F32), 0.0), axis=1, keepdims=True)


EXTRA = 8


def attention_kernel(n, group, tok_rows, me, positions, ids, patches_hbm, qkv_hbm, *refs):
    outs, residual, (patches, qkv, attended, sems) = refs[:n], refs[n:-4], refs[-4:]
    steps = 4
    size = patches.shape[0] // steps
    copies = [
        pltpu.make_async_copy(patches_hbm.at[pl.ds(i * size, size)], patches.at[pl.ds(i * size, size)], sems.at[i])
        for i in range(steps)
    ]
    size = qkv.shape[1] // 2
    copies += [
        pltpu.make_async_copy(
            qkv_hbm.at[i, pl.ds(j * size, size)], qkv.at[i, pl.ds(j * size, size)], sems.at[steps + 2 * i + j]
        )
        for i in range(3)
        for j in range(2)
    ]
    for copy in copies:
        copy.start()
    c = me[0]
    slots, rows = positions.shape[1], ids.shape[1]
    chips, cap, share = n // 2, slots // n, n // 2 // group

    place = positions[...]
    target = jnp.zeros_like(place)
    for i in range(1, n + 1):
        target = target + (place >= i * tok_rows).astype(jnp.int32)
    earlier = lax.broadcasted_iota(jnp.int32, (slots, slots), 0) < lax.broadcasted_iota(jnp.int32, (slots, slots), 1)
    same = as_column(target) == target.astype(F32)
    rank = jnp.sum(jnp.where(earlier & same, 1.0, 0.0), axis=0, keepdims=True).astype(jnp.int32)
    key = jnp.where(target < n, target * cap + rank, -1)

    per = chips * cap
    row = lax.broadcasted_iota(jnp.int32, (n * per, 1), 0)
    receiver = c ^ (row >> log2(per))
    chip = receiver >> 1
    wanted = (((chip ^ ((row & (per - 1)) >> log2(cap))) * 2 + (receiver & 1)) << log2(cap)) + (row & (cap - 1))
    slot_pick = (wanted == key).astype(BF)
    spread = lax.broadcasted_iota(jnp.int32, (slots, rows), 0) == (
        lax.broadcasted_iota(jnp.int32, (slots, rows), 1) >> log2(group)
    )
    offset = chip >> log2(share) == (lax.broadcasted_iota(jnp.int32, (1, rows), 1) & (group - 1))
    select = jnp.where(offset, dot(slot_pick, spread.astype(BF)), 0.0).astype(BF)

    ids_row = ids[...]
    ids_col = as_column(ids_row)
    allowed = (ids_col == ids_row.astype(F32)) & (ids_col >= 0)
    local = (place - target * tok_rows).astype(F32)
    high_digit = jnp.floor(local * (1.0 / 128))
    digits = jnp.concatenate([high_digit, local - high_digit * 128, jnp.zeros((EXTRA - 2, slots), F32)], axis=0)
    taken = jnp.concatenate([slot_pick[i * per : i * per + cap] for i in range(n)], axis=0)
    numbers = nt(digits.astype(BF), taken)
    filled = nt(jnp.ones((EXTRA, slots), BF), taken)
    numbers = jnp.where(filled > 0, numbers, -1.0)
    for copy in copies[:steps]:
        copy.wait()
    x = patches[...]
    heads = []
    for i in range(3):
        for copy in copies[steps + 2 * i : steps + 2 * i + 2]:
            copy.wait()
        heads.append(nt(qkv[i], x).astype(BF))
    q, k, v = heads
    width = qkv.shape[1]
    for h in range(width // HEAD_DIM):
        part = slice(h * HEAD_DIM, (h + 1) * HEAD_DIM)
        scores = lax.dot_general(k[part], q[part], (((0,), (0,)), ((), ())), preferred_element_type=F32)
        scores = jnp.where(allowed, scores * (1.0 / HEAD_DIM**0.5), F32(-1e30))
        weights = jnp.exp(scores - jnp.max(scores, axis=0, keepdims=True))
        total = jnp.sum(weights, axis=0, keepdims=True)
        attended[part] = (dot(v[part], weights.astype(BF)) / total).astype(BF)
    att = attended[...]
    main = width // 128 * 128
    head, tail = att[:main], att[main:]
    no_head, no_tail = jnp.zeros_like(head), jnp.zeros_like(tail)
    left = jnp.concatenate([head, no_head, tail, no_tail], axis=0)
    right = jnp.concatenate([no_head, head, no_tail, tail], axis=0)
    half = per // 2
    for i in range(n):
        low, high = select[i * per : i * per + half], select[i * per + half : (i + 1) * per]
        outs[i][...] = (nt(low, left) + nt(high, right)).astype(BF)

    if share > 1:
        residual[0][...] = dot(select, x).astype(BF)
        residual[1][...] = numbers.astype(BF)
        return
    picked = dot(select, x).astype(BF)
    blank = jnp.zeros((EXTRA, picked.shape[1] - cap), F32)
    for i in range(n):
        residual[i][:per] = picked[i * per : (i + 1) * per]
        tail = jnp.concatenate([numbers[:, i * cap : (i + 1) * cap], blank], axis=1)
        residual[i][per:] = tail.astype(BF)


def attention(patches, window_ids, positions, qkv_weight, c, n, group, tok_rows):
    rows, dv = patches.shape
    slots, width = positions.shape[0], qkv_weight.shape[2]
    per = n // 2 * (slots // n)
    vmem, hbm = pl.BlockSpec(memory_space=pltpu.VMEM), pl.BlockSpec(memory_space=pltpu.HBM)
    if n // 2 // group > 1:
        extra = [jax.ShapeDtypeStruct((n * per, dv), BF), jax.ShapeDtypeStruct((EXTRA, slots), BF)]
    else:
        extra = [jax.ShapeDtypeStruct((per + EXTRA, dv), BF)] * n
    outs = pl.pallas_call(
        functools.partial(attention_kernel, n, group, tok_rows),
        in_specs=[pl.BlockSpec(memory_space=pltpu.SMEM), vmem, vmem, hbm, hbm],
        out_specs=[vmem] * (n + len(extra)),
        out_shape=[jax.ShapeDtypeStruct((per // 2, 2 * width), BF)] * n + extra,
        scratch_shapes=[
            pltpu.VMEM((rows, dv), BF),
            pltpu.VMEM((3, width, dv), BF),
            pltpu.VMEM((width, rows), BF),
            pltpu.SemaphoreType.DMA((10,)),
        ],
        compiler_params=pltpu.CompilerParams(vmem_limit_bytes=61 * 1024 * 1024),
        name="attention",
    )(c.reshape(1), positions[None, :], window_ids[None, :], patches, jnp.swapaxes(qkv_weight, 1, 2))
    return outs[:n], outs[n:]


def stack_kernel(*refs):
    size = refs[0].shape[0]
    for i, ref in enumerate(refs[:-1]):
        refs[-1][i * size : (i + 1) * size] = ref[...]


def stack_rows(blocks):
    rows, cols = blocks[0].shape
    out = jax.ShapeDtypeStruct((len(blocks) * rows, cols), blocks[0].dtype)
    return pl.pallas_call(
        stack_kernel,
        out_shape=out,
        compiler_params=pltpu.CompilerParams(vmem_limit_bytes=4 * 1024 * 1024),
        name="stack_rows",
    )(*blocks)


def project_kernel(n, cap, size, count_pieces, me, *refs):
    refs = list(refs)

    def take(count):
        got = refs[:count]
        del refs[:count]
        return got

    c, t = me[0], me[1]
    chips = n // 2
    half = chips // 2
    slots = n * cap
    atts = take(size + 1 if size == 4 else size)
    pieces = [take(count_pieces), take(count_pieces)]
    patch, merger = take(n), take(2)
    outs, sends, (numbers,) = take(2), take(2), take(1)
    arranged, low, high, hidden, weights, sems = take(6)
    copies = [pltpu.make_async_copy(merger[i], weights.at[i], sems.at[i]) for i in range(2)]
    for copy in copies:
        copy.start()
    piece_rows, cols = pieces[0][0].shape[1:]
    width = count_pieces * piece_rows
    main = width // 128 * 128
    tail = width - main
    core, chip = c & 1, c >> 1
    at = [core * 2 + (chip >> log2(half)), core * 2 + (chip & 1)]
    if count_pieces == 2:
        at = [core, core]
    for side in range(2):
        for place in range(count_pieces):

            def put(side=side, place=place):
                for k in range(count_pieces):
                    start = (place ^ k) * piece_rows
                    for r in range(size):
                        block = pieces[side][k][r]
                        low[side, r, start : start + piece_rows] = block
                        split = min(max(main - start, 0), piece_rows)
                        if split > 0:
                            high[side, r, start : start + split] = block[:split]
                        if split < piece_rows:
                            high[side, r, start + split + tail : start + piece_rows + tail] = block[split:]

            if count_pieces == 1:
                put()
            else:
                pl.when(at[side] == place)(put)
        for r in range(size):
            low[side, r, width:] = jnp.zeros((tail, cols), BF)
            high[side, r, main : main + tail] = jnp.zeros((tail, cols), BF)

    def arrange(r, ref):
        for j in range(half):
            for p in range(n):
                s, to = p ^ (2 * j), (j * n + p) * cap
                arranged[r, to : to + cap] = ref[(s * half + j) * cap : (s * half + j + 1) * cap]

    for r in range(min(size, len(atts) - 1) if size == 4 else size):
        arrange(r, atts[r])
    if size == 4:
        at_end = (t == 0) | (t == size - 1)

        @pl.when(at_end)
        def _():
            arrange(size - 1, atts[size - 1])

        @pl.when(jnp.logical_not(at_end))
        def _():
            arrange(size - 1, atts[size])

    for s in range(n):
        digits = patch[s][chips * cap :, :cap].astype(F32)
        numbers[s : s + 1, :cap] = digits[0:1] * 128 + digits[1:2]
    for side in range(2):
        for h in range(2):
            base = jnp.concatenate(
                [
                    patch[p ^ (2 * j)][(h * half + j) * cap : (h * half + j + 1) * cap, side * cols : (side + 1) * cols]
                    for j in range(half)
                    for p in range(n)
                ],
                axis=0,
            )
            total = base.astype(F32)
            for r in range(size):
                left = jnp.concatenate([arranged[r, :, h * main : (h + 1) * main], arranged[r, :, 2 * main :]], axis=1)
                total = total + dot(left, (low, high)[h][side, r])
            turn = n // 2 * cap if h else 0
            for j in range(half):
                block = total[j * slots : (j + 1) * slots].astype(BF)
                row = (h * half + j) * slots
                if turn:
                    hidden[side, row : row + turn] = block[turn:]
                    hidden[side, row + turn : row + slots] = block[:turn]
                else:
                    hidden[side, row : row + slots] = block
    for copy in copies:
        copy.wait()
    wide = weights.shape[2] // 2
    for own in range(2):

        @pl.when(core == own)
        def _():
            for i, bit in enumerate((1, chips // 2)):
                ids = [r for r in range(chips) if r & bit]
                total = None
                for side in range(2):
                    left = jnp.concatenate([hidden[side, r * slots : (r + 1) * slots] for r in ids], axis=0)
                    part = dot(left, weights[side ^ own, :, i * wide : (i + 1) * wide])
                    total = part if total is None else total + part
                sends[i][...] = total.astype(BF)
            outs[0][...] = hidden[own]
            outs[1][...] = hidden[1 - own]


def project(c, t, atts, pieces, patch, merger, n, cap, size):
    rows = n // 2 * n * cap
    piece_rows, cols = pieces[0][0].shape[1:]
    width = len(pieces[0]) * piece_rows
    deep = 2 * width - width // 128 * 128
    features = merger[0].shape[1]
    vmem, hbm = pl.BlockSpec(memory_space=pltpu.VMEM), pl.BlockSpec(memory_space=pltpu.HBM)
    args = [*atts, *pieces[0], *pieces[1], *patch]
    out_shape = [jax.ShapeDtypeStruct((rows, cols), BF)] * 2
    out_shape += [jax.ShapeDtypeStruct((rows // 2, features // 2), BF)] * 2
    out_shape += [jax.ShapeDtypeStruct((n, 128), F32)]
    return pl.pallas_call(
        functools.partial(project_kernel, n, cap, size, len(pieces[0])),
        in_specs=[pl.BlockSpec(memory_space=pltpu.SMEM)] + [vmem] * len(args) + [hbm, hbm],
        out_specs=[vmem] * len(out_shape),
        out_shape=out_shape,
        scratch_shapes=[
            pltpu.VMEM((size, rows // 2, 2 * width), BF),
            pltpu.VMEM((2, size, deep, cols), BF),
            pltpu.VMEM((2, size, deep, cols), BF),
            pltpu.VMEM((2, rows, cols), BF),
            pltpu.VMEM((2, cols, features), BF),
            pltpu.SemaphoreType.DMA((2,)),
        ],
        compiler_params=pltpu.CompilerParams(vmem_limit_bytes=40 * 1024 * 1024),
        name="project",
    )(jnp.stack([c, t]), *args, *merger)


def columns_kernel(keys, own, other, *outs):
    for out, ids in zip(outs, keys):
        for i, (ref, key) in enumerate([(ref, key) for ref in (own, other) for key in ids]):
            rows = out.shape[1] // (2 * len(ids))
            block = ref[key * rows : (key + 1) * rows].astype(F32)
            out[:, i * rows : (i + 1) * rows] = block.T.astype(BF)


def turned_columns(own, other, keys, slots):
    return pl.pallas_call(
        functools.partial(columns_kernel, keys),
        out_shape=[jax.ShapeDtypeStruct((own.shape[1], 2 * len(k) * slots), BF) for k in keys],
        compiler_params=pltpu.CompilerParams(vmem_limit_bytes=12 * 1024 * 1024),
        name="turned_columns",
    )(own, other)


def accumulate_kernel(tiles, count, *refs):
    left, right, rest = refs[:2], (refs[2 : 2 + count], refs[2 + count : 2 + 2 * count]), refs[2 + 2 * count :]
    step = pl.program_id(0)
    for i in range(2):

        @pl.when(step // tiles == i)
        def _():
            total = dot(left[i][...], jnp.concatenate([r[...] for r in right[i]], axis=0))
            if len(rest) == 2:
                total = total + rest[0][...]
            rest[-1][...] = total


def accumulate(left, right, total):
    out_rows = left[0].shape[0]
    rows, cols = right[0][0].shape
    count = len(right[0])
    tile = min(cols, 512)
    tiles = cols // tile
    whole = pl.BlockSpec(left[0].shape, lambda i: (0, 0))
    low = pl.BlockSpec((rows, tile), lambda i: (0, jnp.minimum(i, tiles - 1)))
    high = pl.BlockSpec((rows, tile), lambda i: (0, jnp.maximum(i - tiles, 0)))
    across = pl.BlockSpec((out_rows, tile), lambda i: (0, i))
    return pl.pallas_call(
        functools.partial(accumulate_kernel, tiles, count),
        grid=(2 * tiles,),
        in_specs=[whole, whole] + [low] * count + [high] * count + ([] if total is None else [across]),
        out_specs=across,
        out_shape=jax.ShapeDtypeStruct((out_rows, 2 * cols), F32),
        compiler_params=pltpu.CompilerParams(vmem_limit_bytes=20 * 1024 * 1024),
    )(*left, *right[0], *right[1], *([] if total is None else [total]))


def gather_tp(x):
    size = lax.axis_size("tp")
    if size != 4:
        return [x] + [swap(x, "tp", r) for r in range(1, size)]
    far, near = swap(x, "tp", 2), swap(x, "tp", 1)
    x, far = lax.optimization_barrier((x, far))
    ends = lax.ppermute(far, "tp", [(1, 0), (2, 3)])
    middle = lax.ppermute(x, "tp", [(1, 2), (2, 1)])
    return [x, near, far, ends, middle]


def sum_tp(x):
    size = lax.axis_size("tp")
    total = x
    for r in range(1, size):
        total = total + swap(x, "tp", r)
    return total


def shards(
    patches, window_ids, positions, text_embed, cotangent, qkv_weight, out_weight, merger_weight, norm_gain
):
    n = lax.axis_size("ctx")
    tp_size = lax.axis_size("tp")
    chips = n // 2
    c, t = lax.axis_index("ctx"), lax.axis_index("tp")
    chip, core = c // 2, c % 2
    slots, tok_rows = positions.shape[0], text_embed.shape[0]
    features = text_embed.shape[1]
    dv = patches.shape[1]
    own_cols = merger_weight.shape[0]
    group = n * own_cols // dv
    share = chips // group
    cap = slots // n
    ctx_bits = [1 << i for i in range((n - 1).bit_length())]
    chip_bits = ctx_bits[:-1]

    blocks, residual = attention(patches, window_ids, positions, qkv_weight, c, n, group, tok_rows)
    att_mine = stack_rows([blocks[0]] + [swap(blocks[s], "ctx", s) for s in range(1, n)])
    att_all = gather_tp(att_mine)

    width, mid = out_weight.shape[0], dv // 2
    count_pieces = 4 if width % 64 == 0 else 2
    piece_rows = width // count_pieces
    if count_pieces == 4:
        at = [core * 2 + chip // (chips // 2), core * 2 + chip % 2]
    else:
        at = [core, core]
    piece = jnp.concatenate(
        [
            lax.dynamic_slice(out_weight, (at[0] * piece_rows, 0), (piece_rows, mid)),
            lax.dynamic_slice(out_weight, (at[1] * piece_rows, mid), (piece_rows, mid)),
        ],
        axis=1,
    )
    stacked = jnp.stack([piece] + [swap(piece, "tp", r) for r in range(1, tp_size)])
    pieces = []
    for i, bit in enumerate((chips, 2)):
        mine = [stacked[:, :, i * mid : (i + 1) * mid]]
        if count_pieces == 4:
            mine.append(swap(mine[0], "ctx", bit))
        pieces.append(mine + [swap(p, "ctx", 1) for p in mine])

    if share > 1:
        picked, numbers = residual
        picked = picked.reshape(n, chips * cap, dv)
        numbers = jnp.moveaxis(numbers.reshape(EXTRA, n, cap), 1, 0)
        numbers = jnp.concatenate([numbers, jnp.zeros((n, EXTRA, 2 * own_cols - cap), BF)], axis=2)
        residual = [
            jnp.concatenate(
                [
                    lax.dynamic_slice_in_dim(picked[r], ((c ^ r) // 2 % share) * 2 * own_cols, 2 * own_cols, 1),
                    numbers[r],
                ]
            )
            for r in range(n)
        ]
        start = (chip % share) * 2 * own_cols
        full = []
        for i in range(2):
            rows = jnp.stack(pieces[i])
            rows = [lax.dynamic_index_in_dim(rows, q ^ at[i], 0, keepdims=False) for q in range(count_pieces)]
            full.append(jnp.concatenate(rows, axis=1))
        full = jnp.concatenate(full, axis=2)
        pieces = [[lax.dynamic_slice_in_dim(full, start + i * own_cols, own_cols, 2)] for i in range(2)]
    patch = [residual[0]] + [swap(residual[s], "ctx", s) for s in range(1, n)]

    merger = [merger_weight, swap(merger_weight, "ctx", 1)]
    hidden_own, hidden_other, *sends, numbers = project(c, t, att_all, pieces, patch, merger, n, cap, tp_size)
    in_rows = numbers[:, :cap].astype(jnp.int32).reshape(-1)
    placed = jnp.arange(tok_rows, dtype=jnp.int32)[:, None] == in_rows[None, :]
    placed_mat = placed.astype(BF)
    is_vision = jnp.any(placed, axis=1)

    half = features // 2
    arrived = []
    for i, bits in enumerate((chip_bits, chip_bits[::-1])):
        bit = bits[0]
        got = swap(sends[i], "ctx", 2 * bit)
        keep_ids = [r for r in range(chips) if not r & bit]
        keep = 0.0
        for side, weight in ((hidden_own, merger[0]), (hidden_other, merger[1])):
            rows = jnp.concatenate([side[r * slots : (r + 1) * slots] for r in keep_ids])
            keep = keep + dot(rows, weight[:, i * half : (i + 1) * half])
        total = {r: (keep + got.astype(F32)).reshape(-1, slots, half)[k] for k, r in enumerate(keep_ids)}
        for bit in bits[1:]:
            keep_ids = [r for r in total if not r & bit]
            send = jnp.stack([total[r | bit] for r in keep_ids]).astype(BF)
            got = swap(send, "ctx", 2 * bit)
            total = {r: total[r] + got[k].astype(F32) for k, r in enumerate(keep_ids)}
        arrived.append(total[0].astype(BF).astype(F32))

    cot_rows = contract_rows(placed_mat, cotangent).astype(BF)

    gain = norm_gain.astype(F32)[None, :]
    text = text_embed.astype(F32)
    gained = gain * cot_rows
    gained = [gained[:, :half], gained[:, half:]]
    gains = [gain[:, :half], gain[:, half:]]
    squares = sum(jnp.sum(x * x, axis=1) for x in arrived)
    inner = sum(jnp.sum(x * g, axis=1) for x, g in zip(arrived, gained))
    sums = sum_tp(jnp.concatenate([jnp.sum(text * text, axis=1), squares, inner]).reshape(-1, 128)).reshape(-1)
    text_scale = lax.rsqrt(sums[:tok_rows] / D + 1e-06)[:, None]
    scale = lax.rsqrt(sums[tok_rows : tok_rows + slots] / D + 1e-06)[:, None]
    inner = sums[tok_rows + slots :][:, None]
    d_rows = [(scale * g - x * scale**3 * inner / D).astype(BF) for x, g in zip(arrived, gained)]
    rows = jnp.concatenate([(x * scale * g).astype(BF) for x, g in zip(arrived, gains)], axis=1)
    vision = dot(placed_mat, rows)
    normed = jnp.where(is_vision[:, None], vision, text * text_scale * gain).astype(BF)

    blocks = [{0: d_rows[0]}, {0: d_rows[1]}]
    for step in range(len(chip_bits)):
        early = [dict(b) for b in blocks]
        for i, bits in enumerate((chip_bits[::-1], chip_bits)):
            bit = bits[step]
            for k in list(blocks[i]):
                blocks[i][k ^ bit] = swap(blocks[i][k], "ctx", 2 * bit)
    late = [{k: v for k, v in b.items() if k not in e} for b, e in zip(blocks, early)]
    keys = [list(part) for parts in (early, late) for part in parts]
    turned = turned_columns(hidden_own, swap(hidden_other, "ctx", 1), keys, slots)
    merger_grad = None
    for parts, left in ((early, turned[:2]), (late, turned[2:])):
        right = []
        for part in parts:
            mine = list(part.values())
            right.append(mine + [swap(b, "ctx", 1) for b in part.values()])
        merger_grad = accumulate(left, right, merger_grad)
    return (normed, merger_grad)


def solution(mesh):
    in_specs = (
        P("ctx", None),
        P("ctx"),
        P("ctx"),
        P("ctx", "tp"),
        P("ctx", "tp"),
        P(None, None, "tp"),
        P("tp", None),
        P("ctx", "tp"),
        P("tp"),
    )
    out_specs = (P("ctx", "tp"), P("ctx", "tp"))
    return jax.shard_map(shards, mesh=mesh, in_specs=in_specs, out_specs=out_specs, check_vma=False)
```

```python
import functools

import jax
import jax.numpy as jnp
from jax import lax
from jax.experimental import pallas as pl
from jax.experimental.pallas import tpu as pltpu
from jax.sharding import PartitionSpec as P


D = 8192
HEAD_DIM = 80
BF = jnp.bfloat16
F32 = jnp.float32


def dot(a, b):
    return jnp.dot(a, b, preferred_element_type=F32)


def contract_rows(left, right):
    return lax.dot_general(left, right, (((0,), (0,)), ((), ())), preferred_element_type=F32)


def swap(x, axis, mask):
    size = lax.axis_size(axis)
    return lax.ppermute(x, axis, [(i, i ^ mask) for i in range(size)])


def nt(a, b):
    return lax.dot_general(a, b, (((1,), (1,)), ((), ())), preferred_element_type=F32)


def log2(size):
    assert size & (size - 1) == 0
    return size.bit_length() - 1


def as_column(row):
    size = row.shape[1]
    eye = lax.broadcasted_iota(jnp.int32, (size, size), 0) == lax.broadcasted_iota(jnp.int32, (size, size), 1)
    return jnp.sum(jnp.where(eye, row.astype(F32), 0.0), axis=1, keepdims=True)


EXTRA = 8


def attention_kernel(n, group, tok_rows, me, positions, ids, patches_hbm, qkv_hbm, *refs):
    outs, residual, (patches, qkv, attended, sems) = refs[:n], refs[n:-4], refs[-4:]
    steps = 4
    size = patches.shape[0] // steps
    copies = [
        pltpu.make_async_copy(patches_hbm.at[pl.ds(i * size, size)], patches.at[pl.ds(i * size, size)], sems.at[i])
        for i in range(steps)
    ]
    size = qkv.shape[1] // 2
    copies += [
        pltpu.make_async_copy(
            qkv_hbm.at[i, pl.ds(j * size, size)], qkv.at[i, pl.ds(j * size, size)], sems.at[steps + 2 * i + j]
        )
        for i in range(3)
        for j in range(2)
    ]
    for copy in copies:
        copy.start()
    c = me[0]
    slots, rows = positions.shape[1], ids.shape[1]
    chips, cap, share = n // 2, slots // n, n // 2 // group

    place = positions[...]
    target = jnp.zeros_like(place)
    for i in range(1, n + 1):
        target = target + (place >= i * tok_rows).astype(jnp.int32)
    earlier = lax.broadcasted_iota(jnp.int32, (slots, slots), 0) < lax.broadcasted_iota(jnp.int32, (slots, slots), 1)
    same = as_column(target) == target.astype(F32)
    rank = jnp.sum(jnp.where(earlier & same, 1.0, 0.0), axis=0, keepdims=True).astype(jnp.int32)
    key = jnp.where(target < n, target * cap + rank, -1)

    per = chips * cap
    row = lax.broadcasted_iota(jnp.int32, (n * per, 1), 0)
    receiver = c ^ (row >> log2(per))
    chip = receiver >> 1
    wanted = (((chip ^ ((row & (per - 1)) >> log2(cap))) * 2 + (receiver & 1)) << log2(cap)) + (row & (cap - 1))
    slot_pick = (wanted == key).astype(BF)
    spread = lax.broadcasted_iota(jnp.int32, (slots, rows), 0) == (
        lax.broadcasted_iota(jnp.int32, (slots, rows), 1) >> log2(group)
    )
    offset = chip >> log2(share) == (lax.broadcasted_iota(jnp.int32, (1, rows), 1) & (group - 1))
    select = jnp.where(offset, dot(slot_pick, spread.astype(BF)), 0.0).astype(BF)

    ids_row = ids[...]
    ids_col = as_column(ids_row)
    allowed = (ids_col == ids_row.astype(F32)) & (ids_col >= 0)
    local = (place - target * tok_rows).astype(F32)
    high_digit = jnp.floor(local * (1.0 / 128))
    digits = jnp.concatenate([high_digit, local - high_digit * 128, jnp.zeros((EXTRA - 2, slots), F32)], axis=0)
    taken = jnp.concatenate([slot_pick[i * per : i * per + cap] for i in range(n)], axis=0)
    numbers = nt(digits.astype(BF), taken)
    filled = nt(jnp.ones((EXTRA, slots), BF), taken)
    numbers = jnp.where(filled > 0, numbers, -1.0)
    for copy in copies[:steps]:
        copy.wait()
    x = patches[...]
    heads = []
    for i in range(3):
        for copy in copies[steps + 2 * i : steps + 2 * i + 2]:
            copy.wait()
        heads.append(nt(qkv[i], x).astype(BF))
    q, k, v = heads
    width = qkv.shape[1]
    for h in range(width // HEAD_DIM):
        part = slice(h * HEAD_DIM, (h + 1) * HEAD_DIM)
        scores = lax.dot_general(k[part], q[part], (((0,), (0,)), ((), ())), preferred_element_type=F32)
        scores = jnp.where(allowed, scores * (1.0 / HEAD_DIM**0.5), F32(-1e30))
        weights = jnp.exp(scores - jnp.max(scores, axis=0, keepdims=True))
        total = jnp.sum(weights, axis=0, keepdims=True)
        attended[part] = (dot(v[part], weights.astype(BF)) / total).astype(BF)
    att = attended[...]
    main = width // 128 * 128
    head, tail = att[:main], att[main:]
    no_head, no_tail = jnp.zeros_like(head), jnp.zeros_like(tail)
    left = jnp.concatenate([head, no_head, tail, no_tail], axis=0)
    right = jnp.concatenate([no_head, head, no_tail, tail], axis=0)
    half = per // 2
    for i in range(n):
        low, high = select[i * per : i * per + half], select[i * per + half : (i + 1) * per]
        outs[i][...] = (nt(low, left) + nt(high, right)).astype(BF)

    if share > 1:
        residual[0][...] = dot(select, x).astype(BF)
        residual[1][...] = numbers.astype(BF)
        return
    picked = dot(select, x).astype(BF)
    blank = jnp.zeros((EXTRA, picked.shape[1] - cap), F32)
    for i in range(n):
        residual[i][:per] = picked[i * per : (i + 1) * per]
        tail = jnp.concatenate([numbers[:, i * cap : (i + 1) * cap], blank], axis=1)
        residual[i][per:] = tail.astype(BF)


def attention(patches, window_ids, positions, qkv_weight, c, n, group, tok_rows):
    rows, dv = patches.shape
    slots, width = positions.shape[0], qkv_weight.shape[2]
    per = n // 2 * (slots // n)
    vmem, hbm = pl.BlockSpec(memory_space=pltpu.VMEM), pl.BlockSpec(memory_space=pltpu.HBM)
    if n // 2 // group > 1:
        extra = [jax.ShapeDtypeStruct((n * per, dv), BF), jax.ShapeDtypeStruct((EXTRA, slots), BF)]
    else:
        extra = [jax.ShapeDtypeStruct((per + EXTRA, dv), BF)] * n
    outs = pl.pallas_call(
        functools.partial(attention_kernel, n, group, tok_rows),
        in_specs=[pl.BlockSpec(memory_space=pltpu.SMEM), vmem, vmem, hbm, hbm],
        out_specs=[vmem] * (n + len(extra)),
        out_shape=[pltpu.VMEM((per // 2, 2 * width), BF)]
        + [jax.ShapeDtypeStruct((per // 2, 2 * width), BF)] * (n - 1)
        + extra,
        scratch_shapes=[
            pltpu.VMEM((rows, dv), BF),
            pltpu.VMEM((3, width, dv), BF),
            pltpu.VMEM((width, rows), BF),
            pltpu.SemaphoreType.DMA((10,)),
        ],
        compiler_params=pltpu.CompilerParams(vmem_limit_bytes=61 * 1024 * 1024),
        name="attention",
    )(c.reshape(1), positions[None, :], window_ids[None, :], patches, jnp.swapaxes(qkv_weight, 1, 2))
    return outs[:n], outs[n:]


def stack_kernel(*refs):
    size = refs[0].shape[0]
    for i, ref in enumerate(refs[:-1]):
        refs[-1][i * size : (i + 1) * size] = ref[...]


def stack_rows(blocks):
    rows, cols = blocks[0].shape
    out = jax.ShapeDtypeStruct((len(blocks) * rows, cols), blocks[0].dtype)
    return pl.pallas_call(
        stack_kernel,
        out_shape=out,
        compiler_params=pltpu.CompilerParams(vmem_limit_bytes=4 * 1024 * 1024),
        name="stack_rows",
    )(*blocks)


def sent_ids(chips, bit):
    return [r for r in range(chips) if r & bit][::-1]


def project_kernel(n, cap, size, count_pieces, me, *refs):
    refs = list(refs)

    def take(count):
        got = refs[:count]
        del refs[:count]
        return got

    c, t = me[0], me[1]
    chips = n // 2
    half = chips // 2
    slots = n * cap
    atts = take(size + 1 if size == 4 else size)
    pieces = [take(count_pieces), take(count_pieces)]
    patch, merger = take(n), take(2)
    outs, sends, (numbers,) = take(2), take(chips), take(1)
    arranged, low, high, hidden, products, weights, sems = take(7)
    copies = [pltpu.make_async_copy(merger[i], weights.at[i], sems.at[i]) for i in range(2)]
    for copy in copies:
        copy.start()
    piece_rows, cols = pieces[0][0].shape[1:]
    width = count_pieces * piece_rows
    main = width // 128 * 128
    tail = width - main
    core, chip = c & 1, c >> 1
    at = [core * 2 + (chip >> log2(half)), core * 2 + (chip & 1)]
    if count_pieces == 2:
        at = [core, core]
    for side in range(2):
        for place in range(count_pieces):

            def put(side=side, place=place):
                for k in range(count_pieces):
                    start = (place ^ k) * piece_rows
                    for r in range(size):
                        block = pieces[side][k][r]
                        low[side, r, start : start + piece_rows] = block
                        split = min(max(main - start, 0), piece_rows)
                        if split > 0:
                            high[side, r, start : start + split] = block[:split]
                        if split < piece_rows:
                            high[side, r, start + split + tail : start + piece_rows + tail] = block[split:]

            if count_pieces == 1:
                put()
            else:
                pl.when(at[side] == place)(put)
        for r in range(size):
            low[side, r, width:] = jnp.zeros((tail, cols), BF)
            high[side, r, main : main + tail] = jnp.zeros((tail, cols), BF)

    def arrange(r, ref):
        for j in range(half):
            for p in range(n):
                s, to = p ^ (2 * j), (j * n + p) * cap
                arranged[r, to : to + cap] = ref[(s * half + j) * cap : (s * half + j + 1) * cap]

    for r in range(min(size, len(atts) - 1) if size == 4 else size):
        arrange(r, atts[r])
    if size == 4:
        at_end = (t == 0) | (t == size - 1)

        @pl.when(at_end)
        def _():
            arrange(size - 1, atts[size - 1])

        @pl.when(jnp.logical_not(at_end))
        def _():
            arrange(size - 1, atts[size])

    for s in range(n):
        digits = patch[s][chips * cap :, :cap].astype(F32)
        numbers[s : s + 1, :cap] = digits[0:1] * 128 + digits[1:2]
    for side in range(2):
        for h in range(2):
            base = jnp.concatenate(
                [
                    patch[p ^ (2 * j)][(h * half + j) * cap : (h * half + j + 1) * cap, side * cols : (side + 1) * cols]
                    for j in range(half)
                    for p in range(n)
                ],
                axis=0,
            )
            total = base.astype(F32)
            for r in range(size):
                left = jnp.concatenate([arranged[r, :, h * main : (h + 1) * main], arranged[r, :, 2 * main :]], axis=1)
                total = total + dot(left, (low, high)[h][side, r])
            turn = n // 2 * cap if h else 0
            for j in range(half):
                block = total[j * slots : (j + 1) * slots].astype(BF)
                row = (h * half + j) * slots
                if turn:
                    hidden[side, row : row + turn] = block[turn:]
                    hidden[side, row + turn : row + slots] = block[:turn]
                else:
                    hidden[side, row : row + slots] = block
    for copy in copies:
        copy.wait()
    wide = weights.shape[2] // 2
    away = [
        pltpu.make_async_copy(products.at[i, pl.ds(k * slots, slots)], sends[i * half + k], sems.at[2 + i * half + k])
        for i in range(2)
        for k in range(half)
    ]
    for own in range(2):

        @pl.when(core == own)
        def _():
            kept = [pltpu.make_async_copy(hidden.at[own ^ i], outs[i], sems.at[2 + chips + i]) for i in range(2)]
            for copy in kept:
                copy.start()
            for i, bit in enumerate((1, chips // 2)):
                ids = sent_ids(chips, bit)
                total = None
                for side in range(2):
                    left = jnp.concatenate([hidden[side, r * slots : (r + 1) * slots] for r in ids], axis=0)
                    part = dot(left, weights[side ^ own, :, i * wide : (i + 1) * wide])
                    total = part if total is None else total + part
                products[i] = total.astype(BF)
                for k in range(len(ids)):
                    away[i * len(ids) + k].start()
            for copy in kept:
                copy.wait()

    for copy in away:
        copy.wait()


def project(c, t, atts, pieces, patch, merger, n, cap, size):
    rows = n // 2 * n * cap
    piece_rows, cols = pieces[0][0].shape[1:]
    width = len(pieces[0]) * piece_rows
    deep = 2 * width - width // 128 * 128
    features = merger[0].shape[1]
    vmem, hbm = pl.BlockSpec(memory_space=pltpu.VMEM), pl.BlockSpec(memory_space=pltpu.HBM)
    args = [*atts, *pieces[0], *pieces[1], *patch]
    out_shape = [pltpu.HBM((rows, cols), BF)] * 2
    out_shape += [pltpu.HBM((n * cap, features // 2), BF)] * (n // 2)
    out_shape += [jax.ShapeDtypeStruct((n, 128), F32)]
    return pl.pallas_call(
        functools.partial(project_kernel, n, cap, size, len(pieces[0])),
        in_specs=[pl.BlockSpec(memory_space=pltpu.SMEM)] + [vmem] * len(args) + [hbm, hbm],
        out_specs=[hbm] * (len(out_shape) - 1) + [vmem],
        out_shape=out_shape,
        scratch_shapes=[
            pltpu.VMEM((size, rows // 2, 2 * width), BF),
            pltpu.VMEM((2, size, deep, cols), BF),
            pltpu.VMEM((2, size, deep, cols), BF),
            pltpu.VMEM((2, rows, cols), BF),
            pltpu.VMEM((2, rows // 2, features // 2), BF),
            pltpu.VMEM((2, cols, features), BF),
            pltpu.SemaphoreType.DMA((4 + n // 2,)),
        ],
        compiler_params=pltpu.CompilerParams(vmem_limit_bytes=24 * 1024 * 1024),
        name="project",
    )(jnp.stack([c, t]), *args, *merger)


def columns_kernel(keys, own, other, *outs):
    for out, ids in zip(outs, keys):
        for i, (ref, key) in enumerate([(ref, key) for ref in (own, other) for key in ids]):
            rows = out.shape[1] // (2 * len(ids))
            block = ref[key * rows : (key + 1) * rows].astype(F32)
            out[:, i * rows : (i + 1) * rows] = block.T.astype(BF)


def turned_columns(own, other, keys, slots):
    return pl.pallas_call(
        functools.partial(columns_kernel, keys),
        out_shape=[jax.ShapeDtypeStruct((own.shape[1], 2 * len(k) * slots), BF) for k in keys],
        compiler_params=pltpu.CompilerParams(vmem_limit_bytes=12 * 1024 * 1024),
        name="turned_columns",
    )(own, other)


def accumulate_kernel(tiles, count, *refs):
    left, right, rest = refs[:2], (refs[2 : 2 + count], refs[2 + count : 2 + 2 * count]), refs[2 + 2 * count :]
    step = pl.program_id(0)
    for i in range(2):

        @pl.when(step // tiles == i)
        def _():
            total = dot(left[i][...], jnp.concatenate([r[...] for r in right[i]], axis=0))
            if len(rest) == 2:
                rest[1][...] = total + rest[0][:, pl.ds(pl.multiple_of(step * total.shape[1], 128), total.shape[1])]
            else:
                rest[0][:, pl.ds(pl.multiple_of(step * total.shape[1], 128), total.shape[1])] = total


def accumulate(left, right, total):
    out_rows = left[0].shape[0]
    rows, cols = right[0][0].shape
    count = len(right[0])
    tile = min(cols, 512)
    tiles = cols // tile
    whole = pl.BlockSpec(left[0].shape, lambda i: (0, 0))
    low = pl.BlockSpec((rows, tile), lambda i: (0, jnp.minimum(i, tiles - 1)))
    high = pl.BlockSpec((rows, tile), lambda i: (0, jnp.maximum(i - tiles, 0)))
    across = pl.BlockSpec((out_rows, tile), lambda i: (0, i))
    return pl.pallas_call(
        functools.partial(accumulate_kernel, tiles, count),
        grid=(2 * tiles,),
        in_specs=[whole, whole] + [low] * count + [high] * count + ([] if total is None else [pl.BlockSpec(memory_space=pltpu.VMEM)]),
        out_specs=pl.BlockSpec(memory_space=pltpu.VMEM) if total is None else across,
        out_shape=(pltpu.VMEM if total is None else jax.ShapeDtypeStruct)((out_rows, 2 * cols), F32),
        compiler_params=pltpu.CompilerParams(vmem_limit_bytes=20 * 1024 * 1024),
    )(*left, *right[0], *right[1], *([] if total is None else [total]))


def gather_tp(x):
    size = lax.axis_size("tp")
    if size != 4:
        return [x] + [swap(x, "tp", r) for r in range(1, size)]
    far, near = swap(x, "tp", 2), swap(x, "tp", 1)
    x, far = lax.optimization_barrier((x, far))
    ends = lax.ppermute(far, "tp", [(1, 0), (2, 3)])
    middle = lax.ppermute(x, "tp", [(1, 2), (2, 1)])
    return [x, near, far, ends, middle]


def sum_tp(x):
    size = lax.axis_size("tp")
    total = x
    for r in range(1, size):
        total = total + swap(x, "tp", r)
    return total


def shards(
    patches, window_ids, positions, text_embed, cotangent, qkv_weight, out_weight, merger_weight, norm_gain
):
    n = lax.axis_size("ctx")
    tp_size = lax.axis_size("tp")
    chips = n // 2
    c, t = lax.axis_index("ctx"), lax.axis_index("tp")
    chip, core = c // 2, c % 2
    slots, tok_rows = positions.shape[0], text_embed.shape[0]
    features = text_embed.shape[1]
    dv = patches.shape[1]
    own_cols = merger_weight.shape[0]
    group = n * own_cols // dv
    share = chips // group
    cap = slots // n
    ctx_bits = [1 << i for i in range((n - 1).bit_length())]
    chip_bits = ctx_bits[:-1]

    blocks, residual = attention(patches, window_ids, positions, qkv_weight, c, n, group, tok_rows)
    att_mine = stack_rows([blocks[0]] + [swap(blocks[s], "ctx", s) for s in range(1, n)])
    att_all = gather_tp(att_mine)

    width, mid = out_weight.shape[0], dv // 2
    count_pieces = 4 if width % 64 == 0 else 2
    piece_rows = width // count_pieces
    if count_pieces == 4:
        at = [core * 2 + chip // (chips // 2), core * 2 + chip % 2]
    else:
        at = [core, core]
    piece = jnp.concatenate(
        [
            lax.dynamic_slice(out_weight, (at[0] * piece_rows, 0), (piece_rows, mid)),
            lax.dynamic_slice(out_weight, (at[1] * piece_rows, mid), (piece_rows, mid)),
        ],
        axis=1,
    )
    stacked = jnp.stack([piece] + [swap(piece, "tp", r) for r in range(1, tp_size)])
    pieces = []
    for i, bit in enumerate((chips, 2)):
        mine = [stacked[:, :, i * mid : (i + 1) * mid]]
        if count_pieces == 4:
            mine.append(swap(mine[0], "ctx", bit))
        pieces.append(mine + [swap(p, "ctx", 1) for p in mine])

    if share > 1:
        picked, numbers = residual
        picked = picked.reshape(n, chips * cap, dv)
        numbers = jnp.moveaxis(numbers.reshape(EXTRA, n, cap), 1, 0)
        numbers = jnp.concatenate([numbers, jnp.zeros((n, EXTRA, 2 * own_cols - cap), BF)], axis=2)
        residual = [
            jnp.concatenate(
                [
                    lax.dynamic_slice_in_dim(picked[r], ((c ^ r) // 2 % share) * 2 * own_cols, 2 * own_cols, 1),
                    numbers[r],
                ]
            )
            for r in range(n)
        ]
        start = (chip % share) * 2 * own_cols
        full = []
        for i in range(2):
            rows = jnp.stack(pieces[i])
            rows = [lax.dynamic_index_in_dim(rows, q ^ at[i], 0, keepdims=False) for q in range(count_pieces)]
            full.append(jnp.concatenate(rows, axis=1))
        full = jnp.concatenate(full, axis=2)
        pieces = [[lax.dynamic_slice_in_dim(full, start + i * own_cols, own_cols, 2)] for i in range(2)]
    patch = [residual[0]] + [swap(residual[s], "ctx", s) for s in range(1, n)]

    merger = [merger_weight, swap(merger_weight, "ctx", 1)]
    hidden_own, hidden_other, *sends, numbers = project(c, t, att_all, pieces, patch, merger, n, cap, tp_size)
    in_rows = numbers[:, :cap].astype(jnp.int32).reshape(-1)
    placed = jnp.arange(tok_rows, dtype=jnp.int32)[:, None] == in_rows[None, :]
    placed_mat = placed.astype(BF)
    is_vision = jnp.any(placed, axis=1)

    half = features // 2
    arrived = []
    for i, bits in enumerate((chip_bits, chip_bits[::-1])):
        bit = bits[0]
        ids = sent_ids(chips, bit)
        sent = dict(zip(ids, sends[i * len(ids) : (i + 1) * len(ids)]))
        keep_ids = [r for r in range(chips) if not r & bit]
        keep = 0.0
        for side, weight in ((hidden_own, merger[0]), (hidden_other, merger[1])):
            rows = jnp.concatenate([side[r * slots : (r + 1) * slots] for r in keep_ids])
            keep = keep + dot(rows, weight[:, i * half : (i + 1) * half])
        total = {r: keep[k * slots : (k + 1) * slots] for k, r in enumerate(keep_ids)}
        for step, bit in enumerate(bits):
            if step:
                sent = {r: total[r].astype(BF) for r in total if r & bit}
            got = {r ^ bit: swap(v, "ctx", 2 * bit) for r, v in sent.items()}
            total = {r: total[r] + got[r].astype(F32) for r in got}
        arrived.append(total[0].astype(BF).astype(F32))

    cot_rows = contract_rows(placed_mat, cotangent).astype(BF)

    gain = norm_gain.astype(F32)[None, :]
    text = text_embed.astype(F32)
    gained = gain * cot_rows
    gained = [gained[:, :half], gained[:, half:]]
    gains = [gain[:, :half], gain[:, half:]]
    squares = sum(jnp.sum(x * x, axis=1) for x in arrived)
    inner = sum(jnp.sum(x * g, axis=1) for x, g in zip(arrived, gained))
    sums = sum_tp(jnp.concatenate([jnp.sum(text * text, axis=1), squares, inner]).reshape(-1, 128)).reshape(-1)
    text_scale = lax.rsqrt(sums[:tok_rows] / D + 1e-06)[:, None]
    scale = lax.rsqrt(sums[tok_rows : tok_rows + slots] / D + 1e-06)[:, None]
    inner = sums[tok_rows + slots :][:, None]
    d_rows = [(scale * g - x * scale**3 * inner / D).astype(BF) for x, g in zip(arrived, gained)]
    rows = jnp.concatenate([(x * scale * g).astype(BF) for x, g in zip(arrived, gains)], axis=1)
    vision = dot(placed_mat, rows)
    normed = jnp.where(is_vision[:, None], vision, text * text_scale * gain).astype(BF)

    blocks = [{0: d_rows[0]}, {0: d_rows[1]}]
    for step in range(len(chip_bits)):
        early = [dict(b) for b in blocks]
        for i, bits in enumerate((chip_bits[::-1], chip_bits)):
            bit = bits[step]
            for k in list(blocks[i]):
                blocks[i][k ^ bit] = swap(blocks[i][k], "ctx", 2 * bit)
    late = [{k: v for k, v in b.items() if k not in e} for b, e in zip(blocks, early)]
    keys = [list(part) for parts in (early, late) for part in parts]
    turned = turned_columns(hidden_own, swap(hidden_other, "ctx", 1), keys, slots)
    merger_grad = None
    for parts, left in ((early, turned[:2]), (late, turned[2:])):
        right = []
        for part in parts:
            mine = list(part.values())
            right.append(mine + [swap(b, "ctx", 1) for b in part.values()])
        merger_grad = accumulate(left, right, merger_grad)
    return (normed, merger_grad)


def solution(mesh):
    in_specs = (
        P("ctx", None),
        P("ctx"),
        P("ctx"),
        P("ctx", "tp"),
        P("ctx", "tp"),
        P(None, None, "tp"),
        P("tp", None),
        P("ctx", "tp"),
        P("tp"),
    )
    out_specs = (P("ctx", "tp"), P("ctx", "tp"))
    return jax.shard_map(shards, mesh=mesh, in_specs=in_specs, out_specs=out_specs, check_vma=False)
```

```python
import functools

import jax
import jax.numpy as jnp
from jax import lax
from jax.experimental import pallas as pl
from jax.experimental.pallas import tpu as pltpu
from jax.sharding import PartitionSpec as P


D = 8192
HEAD_DIM = 80
BF = jnp.bfloat16
F32 = jnp.float32


def dot(a, b):
    return jnp.dot(a, b, preferred_element_type=F32)


def contract_rows(left, right):
    return lax.dot_general(left, right, (((0,), (0,)), ((), ())), preferred_element_type=F32)


def swap(x, axis, mask):
    size = lax.axis_size(axis)
    return lax.ppermute(x, axis, [(i, i ^ mask) for i in range(size)])


def nt(a, b):
    return lax.dot_general(a, b, (((1,), (1,)), ((), ())), preferred_element_type=F32)


def log2(size):
    assert size & (size - 1) == 0
    return size.bit_length() - 1


def as_column(row):
    size = row.shape[1]
    eye = lax.broadcasted_iota(jnp.int32, (size, size), 0) == lax.broadcasted_iota(jnp.int32, (size, size), 1)
    return jnp.sum(jnp.where(eye, row.astype(F32), 0.0), axis=1, keepdims=True)


EXTRA = 8


def attention_kernel(n, group, tok_rows, me, positions, ids, patches_hbm, qkv_hbm, *refs):
    outs, residual, (patches, qkv, attended, sems) = refs[:n], refs[n:-4], refs[-4:]
    steps = 4
    size = patches.shape[0] // steps
    copies = [
        pltpu.make_async_copy(patches_hbm.at[pl.ds(i * size, size)], patches.at[pl.ds(i * size, size)], sems.at[i])
        for i in range(steps)
    ]
    size = qkv.shape[1] // 2
    copies += [
        pltpu.make_async_copy(
            qkv_hbm.at[i, pl.ds(j * size, size)], qkv.at[i, pl.ds(j * size, size)], sems.at[steps + 2 * i + j]
        )
        for i in range(3)
        for j in range(2)
    ]
    for copy in copies:
        copy.start()
    c = me[0]
    slots, rows = positions.shape[1], ids.shape[1]
    chips, cap, share = n // 2, slots // n, n // 2 // group

    place = positions[...]
    target = jnp.zeros_like(place)
    for i in range(1, n + 1):
        target = target + (place >= i * tok_rows).astype(jnp.int32)
    earlier = lax.broadcasted_iota(jnp.int32, (slots, slots), 0) < lax.broadcasted_iota(jnp.int32, (slots, slots), 1)
    same = as_column(target) == target.astype(F32)
    rank = jnp.sum(jnp.where(earlier & same, 1.0, 0.0), axis=0, keepdims=True).astype(jnp.int32)
    key = jnp.where(target < n, target * cap + rank, -1)

    per = chips * cap
    row = lax.broadcasted_iota(jnp.int32, (n * per, 1), 0)
    receiver = c ^ (row >> log2(per))
    chip = receiver >> 1
    wanted = (((chip ^ ((row & (per - 1)) >> log2(cap))) * 2 + (receiver & 1)) << log2(cap)) + (row & (cap - 1))
    slot_pick = (wanted == key).astype(BF)
    spread = lax.broadcasted_iota(jnp.int32, (slots, rows), 0) == (
        lax.broadcasted_iota(jnp.int32, (slots, rows), 1) >> log2(group)
    )
    offset = chip >> log2(share) == (lax.broadcasted_iota(jnp.int32, (1, rows), 1) & (group - 1))
    select = jnp.where(offset, dot(slot_pick, spread.astype(BF)), 0.0).astype(BF)

    ids_row = ids[...]
    ids_col = as_column(ids_row)
    allowed = (ids_col == ids_row.astype(F32)) & (ids_col >= 0)
    local = (place - target * tok_rows).astype(F32)
    high_digit = jnp.floor(local * (1.0 / 128))
    digits = jnp.concatenate([high_digit, local - high_digit * 128, jnp.zeros((EXTRA - 2, slots), F32)], axis=0)
    taken = jnp.concatenate([slot_pick[i * per : i * per + cap] for i in range(n)], axis=0)
    numbers = nt(digits.astype(BF), taken)
    filled = nt(jnp.ones((EXTRA, slots), BF), taken)
    numbers = jnp.where(filled > 0, numbers, -1.0)
    for copy in copies[:steps]:
        copy.wait()
    x = patches[...]
    heads = []
    for i in range(3):
        for copy in copies[steps + 2 * i : steps + 2 * i + 2]:
            copy.wait()
        heads.append(nt(qkv[i], x).astype(BF))
    q, k, v = heads
    width = qkv.shape[1]
    for h in range(width // HEAD_DIM):
        part = slice(h * HEAD_DIM, (h + 1) * HEAD_DIM)
        scores = lax.dot_general(k[part], q[part], (((0,), (0,)), ((), ())), preferred_element_type=F32)
        scores = jnp.where(allowed, scores * (1.0 / HEAD_DIM**0.5), F32(-1e30))
        weights = jnp.exp(scores - jnp.max(scores, axis=0, keepdims=True))
        total = jnp.sum(weights, axis=0, keepdims=True)
        attended[part] = (dot(v[part], weights.astype(BF)) / total).astype(BF)
    att = attended[...]
    main = width // 128 * 128
    head, tail = att[:main], att[main:]
    no_head, no_tail = jnp.zeros_like(head), jnp.zeros_like(tail)
    left = jnp.concatenate([head, no_head, tail, no_tail], axis=0)
    right = jnp.concatenate([no_head, head, no_tail, tail], axis=0)
    half = per // 2
    for i in range(n):
        low, high = select[i * per : i * per + half], select[i * per + half : (i + 1) * per]
        outs[i][...] = (nt(low, left) + nt(high, right)).astype(BF)

    if share > 1:
        residual[0][...] = dot(select, x).astype(BF)
        residual[1][...] = numbers.astype(BF)
        return
    picked = dot(select, x).astype(BF)
    blank = jnp.zeros((EXTRA, picked.shape[1] - cap), F32)
    for i in range(n):
        residual[i][:per] = picked[i * per : (i + 1) * per]
        tail = jnp.concatenate([numbers[:, i * cap : (i + 1) * cap], blank], axis=1)
        residual[i][per:] = tail.astype(BF)


def attention(patches, window_ids, positions, qkv_weight, c, n, group, tok_rows):
    rows, dv = patches.shape
    slots, width = positions.shape[0], qkv_weight.shape[2]
    per = n // 2 * (slots // n)
    vmem, hbm = pl.BlockSpec(memory_space=pltpu.VMEM), pl.BlockSpec(memory_space=pltpu.HBM)
    if n // 2 // group > 1:
        extra = [jax.ShapeDtypeStruct((n * per, dv), BF), jax.ShapeDtypeStruct((EXTRA, slots), BF)]
    else:
        extra = [jax.ShapeDtypeStruct((per + EXTRA, dv), BF)] * n
    outs = pl.pallas_call(
        functools.partial(attention_kernel, n, group, tok_rows),
        in_specs=[pl.BlockSpec(memory_space=pltpu.SMEM), vmem, vmem, hbm, hbm],
        out_specs=[vmem] * (n + len(extra)),
        out_shape=[pltpu.VMEM((per // 2, 2 * width), BF)]
        + [jax.ShapeDtypeStruct((per // 2, 2 * width), BF)] * (n - 1)
        + extra,
        scratch_shapes=[
            pltpu.VMEM((rows, dv), BF),
            pltpu.VMEM((3, width, dv), BF),
            pltpu.VMEM((width, rows), BF),
            pltpu.SemaphoreType.DMA((10,)),
        ],
        compiler_params=pltpu.CompilerParams(vmem_limit_bytes=61 * 1024 * 1024),
        name="attention",
    )(c.reshape(1), positions[None, :], window_ids[None, :], patches, jnp.swapaxes(qkv_weight, 1, 2))
    return outs[:n], outs[n:]


def stack_kernel(*refs):
    size = refs[0].shape[0]
    for i, ref in enumerate(refs[:-1]):
        refs[-1][i * size : (i + 1) * size] = ref[...]


def stack_rows(blocks):
    rows, cols = blocks[0].shape
    out = jax.ShapeDtypeStruct((len(blocks) * rows, cols), blocks[0].dtype)
    return pl.pallas_call(
        stack_kernel,
        out_shape=out,
        compiler_params=pltpu.CompilerParams(vmem_limit_bytes=4 * 1024 * 1024),
        name="stack_rows",
    )(*blocks)


def sent_ids(chips, bit):
    return [r for r in range(chips) if r & bit][::-1]


def taker(refs):
    refs = list(refs)

    def take(count):
        got = refs[:count]
        del refs[:count]
        return got

    return take


def arrange(to, ref, n, cap):
    half = n // 4
    for j in range(half):
        for p in range(n):
            s, row = p ^ (2 * j), (j * n + p) * cap
            to[row : row + cap] = ref[(s * half + j) * cap : (s * half + j + 1) * cap]


def half_rows(arranged, h, main):
    return jnp.concatenate([arranged[:, h * main : (h + 1) * main], arranged[:, 2 * main :]], axis=1)


def start_kernel(n, size, count_pieces, cap, me, *refs):
    take = taker(refs)
    c = me[0]
    atts = take(size - 1)
    pieces = [take(count_pieces), take(count_pieces)]
    merger = take(2)
    (so_far, last), weights = take(2), take(2)
    arranged, low, high, sems = take(4)
    copies = [pltpu.make_async_copy(merger[i], weights[i], sems.at[i]) for i in range(2)]
    for copy in copies:
        copy.start()
    piece_rows, cols = pieces[0][0].shape[1:]
    width = count_pieces * piece_rows
    main = width // 128 * 128
    tail = width - main
    core, chip = c & 1, c >> 1
    at = [core * 2 + (chip >> log2(n // 4)), core * 2 + (chip & 1)]
    if count_pieces == 2:
        at = [core, core]

    def store(h, side, r, start, block):
        if r == size - 1:
            last[h, side, start : start + block.shape[0]] = block
        else:
            (low, high)[h][side, r, start : start + block.shape[0]] = block

    for side in range(2):
        for place in range(count_pieces):

            def put(side=side, place=place):
                for k in range(count_pieces):
                    start = (place ^ k) * piece_rows
                    for r in range(size):
                        block = pieces[side][k][r]
                        store(0, side, r, start, block)
                        split = min(max(main - start, 0), piece_rows)
                        if split > 0:
                            store(1, side, r, start, block[:split])
                        if split < piece_rows:
                            store(1, side, r, start + split + tail, block[split:])

            if count_pieces == 1:
                put()
            else:
                pl.when(at[side] == place)(put)
        for r in range(size):
            store(0, side, r, width, jnp.zeros((tail, cols), BF))
            store(1, side, r, main, jnp.zeros((tail, cols), BF))
    for r in range(size - 1):
        arrange(arranged.at[r], atts[r], n, cap)
    for side in range(2):
        for h in range(2):
            total = None
            for r in range(size - 1):
                part = dot(half_rows(arranged.at[r], h, main), (low, high)[h][side, r])
                total = part if total is None else total + part
            so_far[side, h] = total
    for copy in copies:
        copy.wait()


def project_start(c, atts, pieces, merger, n, cap, size):
    rows, packed = atts[0].shape
    piece_rows, cols = pieces[0][0].shape[1:]
    width = len(pieces[0]) * piece_rows
    deep = 2 * width - width // 128 * 128
    features = merger[0].shape[1]
    vmem, hbm = pl.BlockSpec(memory_space=pltpu.VMEM), pl.BlockSpec(memory_space=pltpu.HBM)
    args = [*atts, *pieces[0], *pieces[1]]
    return pl.pallas_call(
        functools.partial(start_kernel, n, size, len(pieces[0]), cap),
        in_specs=[pl.BlockSpec(memory_space=pltpu.SMEM)] + [vmem] * len(args) + [hbm, hbm],
        out_specs=[vmem] * 4,
        out_shape=[
            pltpu.VMEM((2, 2, rows, cols), F32),
            pltpu.VMEM((2, 2, deep, cols), BF),
            pltpu.VMEM((cols, features), BF),
            pltpu.VMEM((cols, features), BF),
        ],
        scratch_shapes=[
            pltpu.VMEM((size - 1, rows, packed), BF),
            pltpu.VMEM((2, size - 1, deep, cols), BF),
            pltpu.VMEM((2, size - 1, deep, cols), BF),
            pltpu.SemaphoreType.DMA((2,)),
        ],
        compiler_params=pltpu.CompilerParams(vmem_limit_bytes=24 * 1024 * 1024),
        name="project_start",
    )(c.reshape(1), *args, *merger)


def last_kernel(n, size, cap, main, me, *refs):
    take = taker(refs)
    c, t = me[0], me[1]
    chips = n // 2
    half = chips // 2
    slots = n * cap
    atts = take(2 if size == 4 else 1)
    (so_far, last), weights = take(2), take(2)
    patch = take(n)
    outs, sends, (numbers,) = take(2), take(chips), take(1)
    arranged, hidden, products, sems = take(4)
    cols = last.shape[3]
    core = c & 1
    if size == 4:
        at_end = (t == 0) | (t == size - 1)

        @pl.when(at_end)
        def _():
            arrange(arranged, atts[0], n, cap)

        @pl.when(jnp.logical_not(at_end))
        def _():
            arrange(arranged, atts[1], n, cap)

    else:
        arrange(arranged, atts[0], n, cap)
    for s in range(n):
        digits = patch[s][chips * cap :, :cap].astype(F32)
        numbers[s : s + 1, :cap] = digits[0:1] * 128 + digits[1:2]
    for side in range(2):
        for h in range(2):
            base = jnp.concatenate(
                [
                    patch[p ^ (2 * j)][(h * half + j) * cap : (h * half + j + 1) * cap, side * cols : (side + 1) * cols]
                    for j in range(half)
                    for p in range(n)
                ],
                axis=0,
            )
            total = base.astype(F32) + so_far[side, h] + dot(half_rows(arranged, h, main), last[h, side])
            turn = n // 2 * cap if h else 0
            for j in range(half):
                block = total[j * slots : (j + 1) * slots].astype(BF)
                row = (h * half + j) * slots
                if turn:
                    hidden[side, row : row + turn] = block[turn:]
                    hidden[side, row + turn : row + slots] = block[:turn]
                else:
                    hidden[side, row : row + slots] = block
    wide = weights[0].shape[1] // 2
    away = [
        pltpu.make_async_copy(products.at[i, pl.ds(k * slots, slots)], sends[i * half + k], sems.at[2 + i * half + k])
        for i in range(2)
        for k in range(half)
    ]
    for own in range(2):

        @pl.when(core == own)
        def _():
            kept = [pltpu.make_async_copy(hidden.at[own ^ i], outs[i], sems.at[i]) for i in range(2)]
            for copy in kept:
                copy.start()
            for i, bit in enumerate((1, chips // 2)):
                ids = sent_ids(chips, bit)
                total = None
                for side in range(2):
                    left = jnp.concatenate([hidden[side, r * slots : (r + 1) * slots] for r in ids], axis=0)
                    part = dot(left, weights[side ^ own][:, i * wide : (i + 1) * wide])
                    total = part if total is None else total + part
                products[i] = total.astype(BF)
                for k in range(len(ids)):
                    away[i * len(ids) + k].start()
            for copy in kept:
                copy.wait()

    for copy in away:
        copy.wait()


def project_last(c, t, atts, started, patch, n, cap, size, width):
    rows, packed = atts[0].shape
    cols, features = started[2].shape
    vmem, hbm = pl.BlockSpec(memory_space=pltpu.VMEM), pl.BlockSpec(memory_space=pltpu.HBM)
    args = [*atts, *started, *patch]
    out_shape = [pltpu.HBM((2 * rows, cols), BF)] * 2
    out_shape += [pltpu.HBM((n * cap, features // 2), BF)] * (n // 2)
    out_shape += [jax.ShapeDtypeStruct((n, 128), F32)]
    return pl.pallas_call(
        functools.partial(last_kernel, n, size, cap, width // 128 * 128),
        in_specs=[pl.BlockSpec(memory_space=pltpu.SMEM)] + [vmem] * len(args),
        out_specs=[hbm] * (len(out_shape) - 1) + [vmem],
        out_shape=out_shape,
        scratch_shapes=[
            pltpu.VMEM((rows, packed), BF),
            pltpu.VMEM((2, 2 * rows, cols), BF),
            pltpu.VMEM((2, rows, features // 2), BF),
            pltpu.SemaphoreType.DMA((2 + n // 2,)),
        ],
        compiler_params=pltpu.CompilerParams(vmem_limit_bytes=16 * 1024 * 1024),
        name="project_last",
    )(jnp.stack([c, t]), *args)


def columns_kernel(keys, own, other, *outs):
    for out, ids in zip(outs, keys):
        for i, (ref, key) in enumerate([(ref, key) for ref in (own, other) for key in ids]):
            rows = out.shape[1] // (2 * len(ids))
            block = ref[key * rows : (key + 1) * rows].astype(F32)
            out[:, i * rows : (i + 1) * rows] = block.T.astype(BF)


def turned_columns(own, other, keys, slots):
    return pl.pallas_call(
        functools.partial(columns_kernel, keys),
        out_shape=[jax.ShapeDtypeStruct((own.shape[1], 2 * len(k) * slots), BF) for k in keys],
        compiler_params=pltpu.CompilerParams(vmem_limit_bytes=12 * 1024 * 1024),
        name="turned_columns",
    )(own, other)


def accumulate_kernel(tiles, count, *refs):
    left, right, rest = refs[:2], (refs[2 : 2 + count], refs[2 + count : 2 + 2 * count]), refs[2 + 2 * count :]
    step = pl.program_id(0)
    for i in range(2):

        @pl.when(step // tiles == i)
        def _():
            total = dot(left[i][...], jnp.concatenate([r[...] for r in right[i]], axis=0))
            if len(rest) == 2:
                rest[1][...] = total + rest[0][:, pl.ds(pl.multiple_of(step * total.shape[1], 128), total.shape[1])]
            else:
                rest[0][:, pl.ds(pl.multiple_of(step * total.shape[1], 128), total.shape[1])] = total


def accumulate(left, right, total):
    out_rows = left[0].shape[0]
    rows, cols = right[0][0].shape
    count = len(right[0])
    tile = min(cols, 512)
    tiles = cols // tile
    whole = pl.BlockSpec(left[0].shape, lambda i: (0, 0))
    low = pl.BlockSpec((rows, tile), lambda i: (0, jnp.minimum(i, tiles - 1)))
    high = pl.BlockSpec((rows, tile), lambda i: (0, jnp.maximum(i - tiles, 0)))
    across = pl.BlockSpec((out_rows, tile), lambda i: (0, i))
    return pl.pallas_call(
        functools.partial(accumulate_kernel, tiles, count),
        grid=(2 * tiles,),
        in_specs=[whole, whole] + [low] * count + [high] * count + ([] if total is None else [pl.BlockSpec(memory_space=pltpu.VMEM)]),
        out_specs=pl.BlockSpec(memory_space=pltpu.VMEM) if total is None else across,
        out_shape=(pltpu.VMEM if total is None else jax.ShapeDtypeStruct)((out_rows, 2 * cols), F32),
        compiler_params=pltpu.CompilerParams(vmem_limit_bytes=20 * 1024 * 1024),
    )(*left, *right[0], *right[1], *([] if total is None else [total]))


def gather_tp(x):
    size = lax.axis_size("tp")
    if size != 4:
        return [x] + [swap(x, "tp", r) for r in range(1, size)]
    far, near = swap(x, "tp", 2), swap(x, "tp", 1)
    x, far = lax.optimization_barrier((x, far))
    ends = lax.ppermute(far, "tp", [(1, 0), (2, 3)])
    middle = lax.ppermute(x, "tp", [(1, 2), (2, 1)])
    return [x, near, far, ends, middle]


def sum_tp(x):
    size = lax.axis_size("tp")
    total = x
    for r in range(1, size):
        total = total + swap(x, "tp", r)
    return total


def shards(
    patches, window_ids, positions, text_embed, cotangent, qkv_weight, out_weight, merger_weight, norm_gain
):
    n = lax.axis_size("ctx")
    tp_size = lax.axis_size("tp")
    chips = n // 2
    c, t = lax.axis_index("ctx"), lax.axis_index("tp")
    chip, core = c // 2, c % 2
    slots, tok_rows = positions.shape[0], text_embed.shape[0]
    features = text_embed.shape[1]
    dv = patches.shape[1]
    own_cols = merger_weight.shape[0]
    group = n * own_cols // dv
    share = chips // group
    cap = slots // n
    ctx_bits = [1 << i for i in range((n - 1).bit_length())]
    chip_bits = ctx_bits[:-1]

    blocks, residual = attention(patches, window_ids, positions, qkv_weight, c, n, group, tok_rows)
    att_mine = stack_rows([blocks[0]] + [swap(blocks[s], "ctx", s) for s in range(1, n)])
    att_all = gather_tp(att_mine)

    width, mid = out_weight.shape[0], dv // 2
    count_pieces = 4 if width % 64 == 0 else 2
    piece_rows = width // count_pieces
    if count_pieces == 4:
        at = [core * 2 + chip // (chips // 2), core * 2 + chip % 2]
    else:
        at = [core, core]
    piece = jnp.concatenate(
        [
            lax.dynamic_slice(out_weight, (at[0] * piece_rows, 0), (piece_rows, mid)),
            lax.dynamic_slice(out_weight, (at[1] * piece_rows, mid), (piece_rows, mid)),
        ],
        axis=1,
    )
    stacked = jnp.stack([piece] + [swap(piece, "tp", r) for r in range(1, tp_size)])
    pieces = []
    for i, bit in enumerate((chips, 2)):
        mine = [stacked[:, :, i * mid : (i + 1) * mid]]
        if count_pieces == 4:
            mine.append(swap(mine[0], "ctx", bit))
        pieces.append(mine + [swap(p, "ctx", 1) for p in mine])

    if share > 1:
        picked, numbers = residual
        picked = picked.reshape(n, chips * cap, dv)
        numbers = jnp.moveaxis(numbers.reshape(EXTRA, n, cap), 1, 0)
        numbers = jnp.concatenate([numbers, jnp.zeros((n, EXTRA, 2 * own_cols - cap), BF)], axis=2)
        residual = [
            jnp.concatenate(
                [
                    lax.dynamic_slice_in_dim(picked[r], ((c ^ r) // 2 % share) * 2 * own_cols, 2 * own_cols, 1),
                    numbers[r],
                ]
            )
            for r in range(n)
        ]
        start = (chip % share) * 2 * own_cols
        full = []
        for i in range(2):
            rows = jnp.stack(pieces[i])
            rows = [lax.dynamic_index_in_dim(rows, q ^ at[i], 0, keepdims=False) for q in range(count_pieces)]
            full.append(jnp.concatenate(rows, axis=1))
        full = jnp.concatenate(full, axis=2)
        pieces = [[lax.dynamic_slice_in_dim(full, start + i * own_cols, own_cols, 2)] for i in range(2)]
    patch = [residual[0]] + [swap(residual[s], "ctx", s) for s in range(1, n)]

    merger = [merger_weight, swap(merger_weight, "ctx", 1)]
    started = project_start(c, att_all[: tp_size - 1], pieces, merger, n, cap, tp_size)
    hidden_own, hidden_other, *sends, numbers = project_last(
        c, t, att_all[tp_size - 1 :], started, patch, n, cap, tp_size, width
    )
    merger = started[2:]
    in_rows = numbers[:, :cap].astype(jnp.int32).reshape(-1)
    placed = jnp.arange(tok_rows, dtype=jnp.int32)[:, None] == in_rows[None, :]
    placed_mat = placed.astype(BF)
    is_vision = jnp.any(placed, axis=1)

    half = features // 2
    arrived = []
    for i, bits in enumerate((chip_bits, chip_bits[::-1])):
        bit = bits[0]
        ids = sent_ids(chips, bit)
        sent = dict(zip(ids, sends[i * len(ids) : (i + 1) * len(ids)]))
        keep_ids = [r for r in range(chips) if not r & bit]
        keep = 0.0
        for side, weight in ((hidden_own, merger[0]), (hidden_other, merger[1])):
            rows = jnp.concatenate([side[r * slots : (r + 1) * slots] for r in keep_ids])
            keep = keep + dot(rows, weight[:, i * half : (i + 1) * half])
        total = {r: keep[k * slots : (k + 1) * slots] for k, r in enumerate(keep_ids)}
        for step, bit in enumerate(bits):
            if step:
                sent = {r: total[r].astype(BF) for r in total if r & bit}
            got = {r ^ bit: swap(v, "ctx", 2 * bit) for r, v in sent.items()}
            total = {r: total[r] + got[r].astype(F32) for r in got}
        arrived.append(total[0].astype(BF).astype(F32))

    cot_rows = contract_rows(placed_mat, cotangent).astype(BF)

    gain = norm_gain.astype(F32)[None, :]
    text = text_embed.astype(F32)
    gained = gain * cot_rows
    gained = [gained[:, :half], gained[:, half:]]
    gains = [gain[:, :half], gain[:, half:]]
    squares = sum(jnp.sum(x * x, axis=1) for x in arrived)
    inner = sum(jnp.sum(x * g, axis=1) for x, g in zip(arrived, gained))
    text_squares = jnp.sum(text * text, axis=1)
    sums = sum_tp(jnp.concatenate([text_squares, squares, inner]).reshape(-1, 128)).reshape(-1)
    text_scale = lax.rsqrt(sums[:tok_rows] / D + 1e-06)[:, None]
    scale = lax.rsqrt(sums[tok_rows : tok_rows + slots] / D + 1e-06)[:, None]
    inner = sums[tok_rows + slots :][:, None]
    d_rows = [(scale * g - x * scale**3 * inner / D).astype(BF) for x, g in zip(arrived, gained)]
    rows = jnp.concatenate([(x * scale * g).astype(BF) for x, g in zip(arrived, gains)], axis=1)
    vision = dot(placed_mat, rows)
    normed = jnp.where(is_vision[:, None], vision, text * text_scale * gain).astype(BF)

    blocks = [{0: d_rows[0]}, {0: d_rows[1]}]
    for step in range(len(chip_bits)):
        early = [dict(b) for b in blocks]
        for i, bits in enumerate((chip_bits[::-1], chip_bits)):
            bit = bits[step]
            for k in list(blocks[i]):
                blocks[i][k ^ bit] = swap(blocks[i][k], "ctx", 2 * bit)
    late = [{k: v for k, v in b.items() if k not in e} for b, e in zip(blocks, early)]
    keys = [list(part) for parts in (early, late) for part in parts]
    turned = turned_columns(hidden_own, swap(hidden_other, "ctx", 1), keys, slots)
    merger_grad = None
    for parts, left in ((early, turned[:2]), (late, turned[2:])):
        right = []
        for part in parts:
            mine = list(part.values())
            right.append(mine + [swap(b, "ctx", 1) for b in part.values()])
        merger_grad = accumulate(left, right, merger_grad)
    return (normed, merger_grad)


def solution(mesh):
    in_specs = (
        P("ctx", None),
        P("ctx"),
        P("ctx"),
        P("ctx", "tp"),
        P("ctx", "tp"),
        P(None, None, "tp"),
        P("tp", None),
        P("ctx", "tp"),
        P("tp"),
    )
    out_specs = (P("ctx", "tp"), P("ctx", "tp"))
    return jax.shard_map(shards, mesh=mesh, in_specs=in_specs, out_specs=out_specs, check_vma=False)
```
